32 devices in a mesh: row: 8 (over z, y), col: 4 (over x, core).
Axes of the slice: x: 2, y: 2, z: 4, core: 2. Of those that a mesh axis runs over, the one named last changes fastest.
Arguments:
- tile_basis: bfloat16 [8, 4, 2304, 256], P('row', 'col'), may hold values from -6 to 6
- tile_coeffs: bfloat16 [8, 4, 2304, 256], P('row', 'col'), may hold values from -0.375 to 0.375
- panel_basis: bfloat16 [8, 256, 2304], P('row', 'col'), may hold values from -6 to 6
- panel_coeffs: bfloat16 [8, 256, 2304], P('row', 'col'), may hold values from -0.125 to 0.125
- tile_rank: int32 [8, 4], P('row', 'col'), may hold values from 64 to 256
- target_rank: int32 [8, 4], P('row', 'col'), may hold values from 64 to 256, as said below
- panel_rank: int32 [8], replicated, may hold values from 64 to 256
- owner_row: int32 [4], replicated, may hold values from 0 to 7, as said below
Outputs:
- fresh_basis: bfloat16 [8, 4, 2304, 256], P('row', 'col')
- fresh_coeffs: bfloat16 [8, 4, 2304, 256], P('row', 'col')
The draws below stay inside these ranges and needn't reach their ends.
Inputs may be any that keep to these rules, and one draw needn't show every extreme that they name: `target_rank`: a tile's rank after recompression never exceeds its rank before. `owner_row`: distinct panel tile rows.
All inputs are finite; a program needn't handle non-finite values.
Results may differ from the reference program's by a relative error of at most 0.0068.
Values may be sent and summed in bfloat16 or wider, within the bound.
No kernel may reach another device: no remote copies, remote signals or barrier semaphores. Data moves between devices by JAX's collectives and lax.ppermute only.
A program may use at most 64 MiB of HBM per device.

```python
import math
import jax
import jax.numpy as jnp
from jax import lax

NB = 2304
RMAX = 256
NTR = 8
NTC = 4
N_ROW = 8
N_COL = 4


def rank_pair(key):
    base = jax.random.fold_in(key, 7)
    first_key, second_key, third_key = jax.random.split(base, 3)
    lowest = RMAX // 4
    before = jax.random.randint(first_key, (N_ROW, N_COL), lowest, RMAX + 1).astype(jnp.int32)
    spots = jax.random.randint(third_key, (4,), 0, N_ROW * N_COL).astype(jnp.int32)
    flat_before = before.reshape(-1).at[spots[0]].set(RMAX)
    after = jax.random.randint(second_key, (N_ROW * N_COL,), lowest, flat_before + 1).astype(jnp.int32)
    after = after.at[spots[0]].set(RMAX)
    other = (spots[0] + 1 + spots[1] % (N_ROW * N_COL - 1)) % (N_ROW * N_COL)
    flat_before = flat_before.at[other].set(lowest)
    after = after.at[other].set(lowest)
    return (flat_before.reshape(N_ROW, N_COL), after.reshape(N_ROW, N_COL))


def draw_tile_rank(key, part):
    return rank_pair(key)[0]


def draw_target_rank(key, part):
    return rank_pair(key)[1]


def draw_panel_rank(key, part):
    first_key, second_key = jax.random.split(jax.random.fold_in(key, 11))
    lowest = RMAX // 4
    ranks = jax.random.randint(first_key, (N_ROW,), lowest, RMAX + 1).astype(jnp.int32)
    spots = jax.random.permutation(second_key, N_ROW).astype(jnp.int32)
    ranks = ranks.at[spots[0]].set(RMAX)
    ranks = ranks.at[spots[1]].set(lowest)
    return ranks


def draw_owner_row(key, part):
    order = jax.random.permutation(jax.random.fold_in(key, 13), N_ROW).astype(jnp.int32)
    return order[:N_COL]


def block_scale(key, shape, cuts, smallest, high):
    level = 1.0
    for dim, blocks in cuts:
        steps = jax.random.uniform(jax.random.fold_in(jax.random.fold_in(key, 6), dim), (blocks,), jnp.float32, smallest / len(cuts), high / len(cuts))
        level = level * jnp.repeat(jnp.exp(steps), shape[dim] // blocks).reshape((-1,) + (1,) * (len(shape) - 1 - dim))
    return level


def normal_values(own_key, dims, scale, bound, pieces=(), held_as=jnp.bfloat16):
    drawn = scale * jax.random.normal(own_key, dims, jnp.float32)
    if pieces:
        drawn = drawn * block_scale(own_key, dims, pieces, -0.22, 0.18)
    return jnp.clip(drawn, -bound, bound).astype(held_as)


def setup_inputs(seed: int = 0) -> dict:
    key_of = jax.random.split(jax.random.key(seed), 9)
    tile_basis = normal_values(key_of[0], (NTR, NTC, NB, RMAX), 1.0, 6.0, ((0, 8), (1, 4)))
    tile_coeffs = normal_values(key_of[1], (NTR, NTC, NB, RMAX), RMAX ** -0.5, 0.375, ((0, 8), (1, 4)))
    panel_basis = normal_values(key_of[2], (NTR, RMAX, NB), 1.0, 6.0, ((0, 8), (1, 4)))
    panel_coeffs = normal_values(key_of[3], (NTR, RMAX, NB), ((RMAX * RMAX * NB) ** -0.25), 0.125, ((0, 8), (1, 4)))
    tile_rank = draw_tile_rank(jax.random.fold_in(key_of[8], 71), 0)
    target_rank = draw_target_rank(jax.random.fold_in(key_of[8], 71), 0)
    panel_rank = draw_panel_rank(jax.random.fold_in(key_of[8], 71), 0)
    owner_row = draw_owner_row(jax.random.fold_in(key_of[8], 71), 0)
    return {"tile_basis": tile_basis, "tile_coeffs": tile_coeffs, "panel_basis": panel_basis, "panel_coeffs": panel_coeffs, "tile_rank": tile_rank, "target_rank": target_rank, "panel_rank": panel_rank, "owner_row": owner_row}


def keep_columns(matrix, limit):
    flags = (jnp.arange(matrix.shape[1]) < limit).astype(matrix.dtype)
    return matrix * flags[None, :]

def one_tile(basis, coeffs, left_t, right_t, other_left_t, other_right_t, old_rank, goal_rank, here_rank, there_rank):
    left_u = keep_columns(left_t.T, here_rank)
    left_v = keep_columns(right_t.T, here_rank)
    other_u = keep_columns(other_left_t.T, there_rank)
    other_v = keep_columns(other_right_t.T, there_rank)
    basis = keep_columns(basis, old_rank)
    coeffs = keep_columns(coeffs, old_rank)
    coupling = jnp.dot(left_v.T.astype(jnp.float32), other_v.astype(jnp.float32), preferred_element_type=jnp.float32).astype(jnp.bfloat16)
    shifted = jnp.dot(left_u.astype(jnp.float32), coupling.astype(jnp.float32), preferred_element_type=jnp.float32).astype(jnp.bfloat16)
    first = jnp.concatenate([basis, -shifted], axis=1)
    second = jnp.concatenate([coeffs, other_u], axis=1)
    sketch = keep_columns(coeffs, goal_rank)
    core = jnp.dot(second.T.astype(jnp.float32), sketch.astype(jnp.float32), preferred_element_type=jnp.float32).astype(jnp.bfloat16)
    sampled = jnp.dot(first.astype(jnp.float32), core.astype(jnp.float32), preferred_element_type=jnp.float32)
    extra = (jnp.arange(sampled.shape[1]) >= goal_rank).astype(jnp.float32)
    gram_matrix = jnp.dot(sampled.T.astype(jnp.float32), sampled.astype(jnp.float32), precision=lax.Precision.HIGHEST, preferred_element_type=jnp.float32) + jnp.diag(extra)
    factor = jnp.linalg.cholesky(gram_matrix)
    orthonormal = jax.scipy.linalg.solve_triangular(factor, sampled.T, lower=True).T
    scaling = math.sqrt(NB)
    fresh_basis = (orthonormal * scaling).astype(jnp.bfloat16)
    reduced = (jnp.dot(first.T.astype(jnp.float32), fresh_basis.astype(jnp.float32), preferred_element_type=jnp.float32) / scaling).astype(jnp.bfloat16)
    fresh_coeffs = jnp.dot(second.astype(jnp.float32), reduced.astype(jnp.float32), preferred_element_type=jnp.float32).astype(jnp.bfloat16)
    return (fresh_basis, fresh_coeffs)

def reference(tile_basis, tile_coeffs, panel_basis, panel_coeffs, tile_rank, target_rank, panel_rank, owner_row):

    def single(flat):
        row_at = flat // N_COL
        col_at = flat % N_COL
        source = owner_row[col_at]
        return one_tile(tile_basis[row_at, col_at], tile_coeffs[row_at, col_at], panel_basis[row_at], panel_coeffs[row_at], panel_basis[source], panel_coeffs[source], tile_rank[row_at, col_at], target_rank[row_at, col_at], panel_rank[row_at], panel_rank[source])
    fresh_basis, fresh_coeffs = lax.map(single, jnp.arange(N_ROW * N_COL, dtype=jnp.int32))
    shape_out = (N_ROW, N_COL, NB, RMAX)
    return (fresh_basis.reshape(shape_out), fresh_coeffs.reshape(shape_out))
```

```python
import functools
import math

import jax
import jax.numpy as jnp
from jax import lax
from jax.experimental import pallas as pl
from jax.experimental.pallas import tpu as pltpu
from jax.sharding import PartitionSpec as P

F32 = jnp.float32
BF16 = jnp.bfloat16
HIGHEST = lax.Precision.HIGHEST
VMEM = pl.BlockSpec(memory_space=pltpu.VMEM)
SMEM = pl.BlockSpec(memory_space=pltpu.SMEM)
ANY = pl.BlockSpec(memory_space=pl.ANY)
ROUGH, FINE = 0.05, 2e-3
ROUGH_STEPS, FINE_STEPS = 8, 6


def nn(a, b, precision=None):
    return lax.dot_general(a, b, (((1,), (0,)), ((), ())), precision=precision, preferred_element_type=F32)


def nt(a, b, precision=None):
    return lax.dot_general(a, b, (((1,), (1,)), ((), ())), precision=precision, preferred_element_type=F32)


def tn(a, b, precision=None):
    return lax.dot_general(a, b, (((0,), (0,)), ((), ())), precision=precision, preferred_element_type=F32)


def halves(x):
    high = x.astype(BF16)
    return high, (x - high.astype(F32)).astype(BF16)


def ring_order(n):
    return list(range(0, n, 2)) + list(range(n - 1, 0, -2))


def ring_gather(x, axis, n):
    ring = ring_order(n)
    ahead = [(ring[i], ring[(i + 1) % n]) for i in range(n)]
    back = [(b, a) for a, b in ahead]
    out = [None] * n
    out[0] = right = left = x
    for s in range(1, n // 2):
        right = lax.ppermute(right, axis, ahead)
        left = lax.ppermute(left, axis, back)
        out[s], out[n - s] = right, left
    half = x.shape[0] // 2
    out[n // 2] = (lax.ppermute(right[:half], axis, ahead), lax.ppermute(left[half:], axis, back))
    return out


def swap(x, axis, n, m):
    return lax.ppermute(x, axis, [(i, i ^ m) for i in range(n)])


def xor_gather(x, axis, n):
    have = {0: x}
    bit = n // 2
    while bit:
        for m in list(have):
            have[m | bit] = swap(have[m], axis, n, bit)
        bit //= 2
    return [have[m] for m in range(n)]


def pick_and_multiply(n_row, n_col, count, index, *refs):
    pieces = refs[: n_row + 1]
    rights = refs[n_row + 1 : n_row + 1 + count]
    out_ref, picked, sem = refs[n_row + 1 + count :]
    half = n_row // 2
    low = picked.shape[1] // 2
    for m in range(n_col):
        for k in range(n_row):

            @pl.when(index[m] == k)
            def _():
                if k == half:
                    a = pltpu.make_async_copy(pieces[half], picked.at[m, pl.ds(0, low)], sem.at[m])
                    b = pltpu.make_async_copy(pieces[n_row], picked.at[m, pl.ds(low, low)], sem.at[m])
                    a.start()
                    a.wait()
                    b.start()
                    b.wait()
                else:
                    c = pltpu.make_async_copy(pieces[k], picked.at[m], sem.at[m])
                    c.start()
                    c.wait()
    for m in range(n_col):
        right = rights[m if count > 1 else 0]
        dot = nn if count > 1 else nt
        out_ref[m] = dot(picked[m], right[...]).astype(BF16)


def picked_products(pieces, rights, index, n_row, n_col, name):
    shard, width = pieces[0].shape
    half = n_row // 2
    flat = list(pieces)
    flat[half] = pieces[half][0]
    flat.append(pieces[half][1])
    rank = n_col * shard
    keep = len(rights) > 1
    outs = jax.ShapeDtypeStruct((n_col, shard, rank), BF16)
    sel = jax.ShapeDtypeStruct((n_col, shard, width), BF16)
    return pl.pallas_call(
        functools.partial(pick_and_multiply, n_row, n_col, len(rights)),
        out_shape=(outs, sel),
        in_specs=[SMEM] + [ANY] * len(flat) + [VMEM] * len(rights),
        out_specs=(VMEM, VMEM),
        scratch_shapes=[pltpu.SemaphoreType.DMA((n_col,))],
        compiler_params=pltpu.CompilerParams(vmem_limit_bytes=40 << 20),
        cost_estimate=pl.CostEstimate(
            flops=2 * rank * rank * width, bytes_accessed=6 << 20, transcendentals=0
        ),
        name=name,
    )(index, *flat, *rights)


def lower_half(e, eye, below):
    return jnp.where(below, e, jnp.where(eye, 0.5 * e, 0.0))


def finish(n_col, scalars, u_ref, v_ref, uit_ref, h_ref, cu_ref, *refs):
    ujt_in, kt_in, cl_in = refs[:n_col], refs[n_col : 2 * n_col], refs[2 * n_col : 3 * n_col]
    q_ref, w_ref, ujt, kt, cl, mf, hm, gn, y_ref, a_ref = refs[3 * n_col :]
    rows, rank = u_ref.shape
    shard = rank // n_col
    old, goal, here, there, me = (scalars[t] for t in range(5))
    sub = lax.broadcasted_iota(jnp.int32, (rank, rank), 0)
    lane = lax.broadcasted_iota(jnp.int32, (rank, rank), 1)
    eye, below = sub == lane, sub > lane
    one = jnp.where(eye, 1.0, 0.0).astype(F32)
    for m in range(n_col):
        at = pl.ds(pl.multiple_of((me ^ m) * shard, shard), shard)
        kt[at, :] = kt_in[m][...]
        cl[at, :] = cl_in[m][...]
        ujt[at, :] = ujt_in[m][...]
    zero = jnp.zeros((rank, rank), F32)
    kt[...] = jnp.where((sub < there) & (lane < here), kt[...].astype(F32), zero).astype(BF16)
    cl[...] = jnp.where(lane < goal, cl[...].astype(F32), zero).astype(BF16)
    cu = jnp.where((sub < old) & (lane < goal), cu_ref[...], zero).astype(BF16).astype(F32)
    mf[pl.ds(0, rank), :] = cu
    mf[pl.ds(rank, rank), :] = -tn(kt[...], cl[...])
    hm[...] = nn(h_ref[...], mf[...], HIGHEST)
    g = tn(mf[...], hm[...], HIGHEST) + jnp.where(eye & (lane >= goal), 1.0, 0.0)
    dg = jnp.where(eye, g, 0.0)
    d_row = lax.rsqrt(jnp.sum(dg, axis=0, keepdims=True))
    d_col = lax.rsqrt(jnp.sum(dg, axis=1, keepdims=True))
    gn[...] = g * d_col * d_row
    y_ref[...] = one - lower_half(gn[...] - one, eye, below)
    gb = gn[...].astype(BF16)

    def rough(carry):
        step, _ = carry
        y = y_ref[...]
        yb = y.astype(BF16)
        e = nt(nn(yb, gb).astype(BF16), yb) - one
        y_ref[...] = y - nn(lower_half(e, eye, below).astype(BF16), yb)
        return step + 1, jnp.max(jnp.abs(e))

    def fine(carry):
        step, _ = carry
        y = y_ref[...]
        e = nt(nn(y, gn[...], HIGHEST), y, HIGHEST) - one
        y_ref[...] = y - nn(lower_half(e, eye, below), y, HIGHEST)
        return step + 1, jnp.max(jnp.abs(e))

    lax.while_loop(lambda c: (c[0] < ROUGH_STEPS) & (c[1] > ROUGH), rough, (jnp.int32(0), F32(1.0)))
    _, err = lax.while_loop(lambda c: (c[0] < FINE_STEPS) & (c[1] > FINE), fine, (jnp.int32(0), F32(1.0)))

    lowest = jnp.min(jnp.where(eye, y_ref[...], 1.0))

    @pl.when(jnp.logical_not((err <= FINE) & (lowest > 0.0)))
    def _():
        a_ref[...] = gn[...]
        y_ref[...] = one

        def pivot(k, _):
            col = jnp.sum(jnp.where(lane == k, a_ref[...], 0.0), axis=1, keepdims=True)
            row = jnp.sum(jnp.where(sub == k, a_ref[...], 0.0), axis=0, keepdims=True)
            yrow = jnp.sum(jnp.where(sub == k, y_ref[...], 0.0), axis=0, keepdims=True)
            top = jnp.sum(jnp.where(lax.broadcasted_iota(jnp.int32, (1, rank), 1) == k, row, 0.0))
            inv = 1.0 / jnp.sqrt(jnp.full((1, rank), top))
            row, yrow = row * inv, yrow * inv
            col = jnp.where(lax.broadcasted_iota(jnp.int32, (rank, 1), 0) > k, col * inv[:, :1], 0.0)
            a_ref[...] = a_ref[...] - col * row
            y_ref[...] = jnp.where(sub == k, yrow, y_ref[...] - col * yrow)
            return 0

        lax.fori_loop(0, rank, pivot, 0)

    x = y_ref[...] * d_row
    root = math.sqrt(rows)
    c = nt(mf[...], x, HIGHEST) * root
    r = nt(hm[...], x, HIGHEST)
    r_up = jnp.where(sub < old, r[:rank], 0.0).astype(BF16)
    r_low = (-nn(kt[...].astype(F32), r[rank:], HIGHEST)).astype(BF16)
    ch, cl2 = halves(c)
    cu_h, cu_l, cl_h, cl_l = ch[:rank], cl2[:rank], ch[rank:], cl2[rank:]
    step = 256 if rows % 256 == 0 else rows
    for t in range(rows // step):
        at = pl.ds(t * step, step)
        u, v = u_ref[at, :], v_ref[at, :]
        ui, uj = uit_ref[:, at], ujt[:, at]
        q_ref[at, :] = (nn(u, cu_h) + nn(u, cu_l) + tn(ui, cl_h) + tn(ui, cl_l)).astype(BF16)
        w_ref[at, :] = (nn(v, r_up) + tn(uj, r_low)).astype(BF16)


def body(tile_basis, tile_coeffs, panel_basis, panel_coeffs, tile_rank, target_rank, panel_rank, owner_row):
    n_row, n_col = lax.axis_size("row"), lax.axis_size("col")
    row, col = lax.axis_index("row"), lax.axis_index("col")
    u, v = tile_basis[0, 0], tile_coeffs[0, 0]
    pu, pv = panel_basis[0], panel_coeffs[0]
    rows, rank = u.shape
    shard = rank // n_col

    us = ring_gather(pu, "row", n_row)
    vs = ring_gather(pv, "row", n_row)
    ui_parts = xor_gather(pu, "col", n_col)
    vi_parts = xor_gather(pv, "col", n_col)
    v_tiles = xor_gather(v, "col", n_col)

    place = [0] * n_row
    for at, r in enumerate(ring_order(n_row)):
        place[r] = at
    place = jnp.array(place, jnp.int32)
    columns = col ^ jnp.arange(n_col, dtype=jnp.int32)
    owners = owner_row[columns]
    index = (place[row] - place[owners] + n_row) % n_row

    uit = jnp.zeros((rank, rows), BF16)
    vit = jnp.zeros((rank, rows), BF16)
    for m in range(n_col):
        uit = lax.dynamic_update_slice(uit, ui_parts[m], ((col ^ m) * shard, 0))
        vit = lax.dynamic_update_slice(vit, vi_parts[m], ((col ^ m) * shard, 0))

    h11 = tn(u, u)
    h21 = nn(uit, u)
    h22 = nt(uit, uit)
    h = jnp.concatenate([jnp.concatenate([h11, h21.T], 1), jnp.concatenate([h21, h22], 1)], 0)
    core_up = tn(v, v)

    low, u_sel = picked_products(us, v_tiles, index, n_row, n_col, "core_low")
    kt, _ = picked_products(vs, [vit], index, n_row, n_col, "coupling")
    low = [low[0]] + [swap(low[m], "col", n_col, m) for m in range(1, n_col)]
    kts = [kt[0]] + [swap(kt[m], "col", n_col, m) for m in range(1, n_col)]
    ujs = [u_sel[0]] + [swap(u_sel[m], "col", n_col, m) for m in range(1, n_col)]

    scalars = jnp.stack([tile_rank[0, 0], target_rank[0, 0], panel_rank[row], panel_rank[owners[0]], col])
    out = jax.ShapeDtypeStruct((rows, rank), BF16)
    square = pltpu.VMEM((rank, rank), F32)
    fresh_basis, fresh_coeffs = pl.pallas_call(
        functools.partial(finish, n_col),
        out_shape=(out, out),
        in_specs=[SMEM] + [VMEM] * (5 + 3 * n_col),
        out_specs=(VMEM, VMEM),
        scratch_shapes=[
            pltpu.VMEM((rank, rows), BF16),
            pltpu.VMEM((rank, rank), BF16),
            pltpu.VMEM((rank, rank), BF16),
            pltpu.VMEM((2 * rank, rank), F32),
            pltpu.VMEM((2 * rank, rank), F32),
            square,
            square,
            square,
        ],
        compiler_params=pltpu.CompilerParams(vmem_limit_bytes=48 << 20),
        cost_estimate=pl.CostEstimate(flops=8 << 30, bytes_accessed=12 << 20, transcendentals=0),
        name="finish",
    )(scalars, u, v, uit, h, core_up, *ujs, *kts, *low)
    return fresh_basis[None, None], fresh_coeffs[None, None]


def solution(mesh):
    tiles, panels = P("row", "col", None, None), P("row", "col", None)
    return jax.shard_map(
        body,
        mesh=mesh,
        in_specs=(tiles, tiles, panels, panels, P("row", "col"), P("row", "col"), P(), P()),
        out_specs=(tiles, tiles),
        check_vma=False,
    )
```

```python
import functools
import math

import jax
import jax.numpy as jnp
from jax import lax
from jax.experimental import pallas as pl
from jax.experimental.pallas import tpu as pltpu
from jax.sharding import PartitionSpec as P

F32 = jnp.float32
BF16 = jnp.bfloat16
HIGHEST = lax.Precision.HIGHEST
VMEM = pl.BlockSpec(memory_space=pltpu.VMEM)
SMEM = pl.BlockSpec(memory_space=pltpu.SMEM)
ANY = pl.BlockSpec(memory_space=pl.ANY)
ROUGH, FINE = 0.05, 0.015
ROUGH_STEPS, FINE_STEPS = 12, 6


def nn(a, b, precision=None):
    return lax.dot_general(a, b, (((1,), (0,)), ((), ())), precision=precision, preferred_element_type=F32)


def nt(a, b, precision=None):
    return lax.dot_general(a, b, (((1,), (1,)), ((), ())), precision=precision, preferred_element_type=F32)


def tn(a, b, precision=None):
    return lax.dot_general(a, b, (((0,), (0,)), ((), ())), precision=precision, preferred_element_type=F32)


def halves(x):
    high = x.astype(BF16)
    return high, (x - high.astype(F32)).astype(BF16)


def after(x, *others):
    return lax.optimization_barrier((x, *others))[0]


def ring_place(r, n):
    return jnp.where(r % 2 == 0, r // 2, n - 1 - r // 2)


def ring_steps(n):
    ring = list(range(0, n, 2)) + list(range(n - 1, 0, -2))
    ahead = [(ring[i], ring[(i + 1) % n]) for i in range(n)]
    return ahead, [(b, a) for a, b in ahead]


def ring_gathers(left, right, axis, n, early):
    ahead, back = ring_steps(n)
    send = lambda x, way: lax.ppermute(x, axis, way)
    low = left.shape[0] // 2
    lefts, rights = [left] + [None] * (n - 1), []
    for h in range(2):
        rights.append([right[h * low : (h + 1) * low]] + [None] * (n - 1))

    def right_step(h, s, gate):
        r = rights[h]
        if s < n // 2:
            r[s] = send(after(r[s - 1], *gate), ahead)
            r[n - s] = send(after(r[(n - s + 1) % n], *gate), back)
            return (r[s], r[n - s])
        r[s] = send(after(r[s + 1], *gate), back)
        return (r[s],)

    turns = [(h, s) for s in range(1, n // 2 + 1) for h in range(2)]
    before, beside = (), ()
    for s in range(1, n // 2 + 1):
        gate = beside
        if s >= 3 and early:
            gate = (*gate, *early[0]())
            early = early[1:]
        lefts[s] = send(after(lefts[s - 1], *gate), ahead)
        if s < n // 2:
            lefts[n - s] = send(after(lefts[(n - s + 1) % n], *gate), back)
        if s >= 2:
            beside = right_step(*turns.pop(0), before)
        before = (lefts[s],) if s == n // 2 else (lefts[s], lefts[n - s])
    return lefts, rights, lambda gate: right_rest(turns, right_step, gate)


def right_rest(turns, right_step, gate):
    for at, turn in enumerate(turns):
        right_step(*turn, gate if at else ())


def swap(x, axis, n, m):
    return lax.ppermute(x, axis, [(i, i ^ m) for i in range(n)])


def xor_gather(x, axis, n):
    have = {0: x}
    bit = n // 2
    while bit:
        for m in list(have):
            have[m | bit] = swap(have[m], axis, n, bit)
        bit //= 2
    return [have[m] for m in range(n)]


def owner_steps(n_row, n_col, owner):
    row, col = lax.axis_index("row"), lax.axis_index("col")
    here = ring_place(row, n_row)
    return [lax.rem(here - ring_place(owner[col ^ m], n_row) + n_row, n_row) for m in range(n_col)]


def pick_left(n_row, n_col, owner, *refs):
    pieces, outs, sem = refs[:n_row], refs[n_row:-1], refs[-1]
    steps = owner_steps(n_row, n_col, owner)
    for m in range(n_col):
        for k in range(n_row):

            @pl.when(steps[m] == k)
            def _():
                pltpu.make_async_copy(pieces[k], outs[m], sem.at[m]).start()

    for m in range(n_col):
        pltpu.make_async_copy(pieces[0], outs[m], sem.at[m]).wait()


def picked_left(pieces, owner, n_row, n_col):
    shard, width = pieces[0].shape
    return pl.pallas_call(
        functools.partial(pick_left, n_row, n_col),
        out_shape=[jax.ShapeDtypeStruct((shard, width), BF16)] * n_col,
        in_specs=[SMEM] + [ANY] * n_row,
        out_specs=[VMEM] * n_col,
        scratch_shapes=[pltpu.SemaphoreType.DMA((n_col,))],
        cost_estimate=pl.CostEstimate(flops=0, bytes_accessed=3 << 20, transcendentals=0),
        name="pick_left",
    )(owner, *pieces)


def couple(n_row, n_col, owner, *refs):
    pieces = refs[: 2 * n_row]
    parts = refs[2 * n_row : 2 * n_row + n_col]
    outs = refs[2 * n_row + n_col : 2 * n_row + 2 * n_col]
    picked, mine, sem, sem2 = refs[2 * n_row + 2 * n_col :]
    shard = outs[0].shape[0]
    low = shard // 2
    col = lax.axis_index("col")
    steps = owner_steps(n_row, n_col, owner)

    def copies(m, k):
        return (
            pltpu.make_async_copy(pieces[k], picked.at[pl.ds(m * shard, low)], sem.at[m]),
            pltpu.make_async_copy(pieces[n_row + k], picked.at[pl.ds(m * shard + low, low)], sem2.at[m]),
        )

    for m in range(n_col):
        for k in range(n_row):

            @pl.when(steps[m] == k)
            def _():
                a, b = copies(m, k)
                a.start()
                b.start()

    for m in range(n_col):
        at = pl.ds(pl.multiple_of((col ^ m) * shard, shard), shard)
        mine[at, :] = parts[m][...]
    for m in range(n_col):
        a, b = copies(m, 0)
        a.wait()
        b.wait()
    product = nt(picked[...], mine[...]).astype(BF16)
    for m in range(n_col):
        outs[m][...] = product[m * shard : (m + 1) * shard]


def coupled(halves_, parts, owner, n_row, n_col):
    shard, width = parts[0].shape
    rank = n_col * shard
    return pl.pallas_call(
        functools.partial(couple, n_row, n_col),
        out_shape=[jax.ShapeDtypeStruct((shard, rank), BF16)] * n_col,
        in_specs=[SMEM] + [ANY] * (2 * n_row) + [VMEM] * n_col,
        out_specs=[VMEM] * n_col,
        scratch_shapes=[
            pltpu.VMEM((rank, width), BF16),
            pltpu.VMEM((rank, width), BF16),
            pltpu.SemaphoreType.DMA((n_col,)),
            pltpu.SemaphoreType.DMA((n_col,)),
        ],
        compiler_params=pltpu.CompilerParams(vmem_limit_bytes=32 << 20),
        cost_estimate=pl.CostEstimate(flops=2 * rank * rank * width, bytes_accessed=3 << 20, transcendentals=0),
        name="coupling",
    )(owner, *halves_[0], *halves_[1], *parts)


def grams(n_col, u_ref, v_ref, *refs):
    parts, (uit, h_ref, cu_ref) = refs[:n_col], refs[n_col:]
    rank = cu_ref.shape[0]
    shard = rank // n_col
    col = lax.axis_index("col")
    for m in range(n_col):
        at = pl.ds(pl.multiple_of((col ^ m) * shard, shard), shard)
        uit[at, :] = parts[m][...]
    top, bottom = pl.ds(0, rank), pl.ds(rank, rank)
    cu_ref[...] = tn(v_ref[...], v_ref[...])
    h_ref[top, :rank] = tn(u_ref[...], u_ref[...])
    cross = nn(uit[...], u_ref[...])
    h_ref[bottom, :rank] = cross
    h_ref[top, rank:] = cross.T
    h_ref[bottom, rank:] = nt(uit[...], uit[...])


def gram_products(u, v, parts, n_col):
    rows, rank = u.shape
    return pl.pallas_call(
        functools.partial(grams, n_col),
        out_shape=[
            jax.ShapeDtypeStruct((rank, rows), BF16),
            jax.ShapeDtypeStruct((2 * rank, 2 * rank), F32),
            jax.ShapeDtypeStruct((rank, rank), F32),
        ],
        in_specs=[VMEM] * (2 + n_col),
        out_specs=[VMEM] * 3,
        compiler_params=pltpu.CompilerParams(vmem_limit_bytes=40 << 20),
        cost_estimate=pl.CostEstimate(flops=8 * rank * rank * rows, bytes_accessed=6 << 20, transcendentals=0),
        name="grams",
    )(u, v, *parts)


def lower_half(e, eye, below):
    return jnp.where(below, e, jnp.where(eye, 0.5 * e, 0.0))


def finish(n_col, old_ref, goal_ref, panel, owner, u_ref, v_ref, uit_ref, h_ref, cu_ref, *refs):
    ujt_in, kt_in = refs[:n_col], refs[n_col : 2 * n_col]
    q_ref, w_ref, ujt, kt, mf, hm, gn, y_ref, a_ref = refs[2 * n_col :]
    rows, rank = u_ref.shape
    shard = rank // n_col
    row, col = lax.axis_index("row"), lax.axis_index("col")
    old, goal, here, there = old_ref[0, 0], goal_ref[0, 0], panel[row], panel[owner[col]]
    sub = lax.broadcasted_iota(jnp.int32, (rank, rank), 0)
    lane = lax.broadcasted_iota(jnp.int32, (rank, rank), 1)
    eye, below = sub == lane, sub > lane
    one = jnp.where(eye, 1.0, 0.0).astype(F32)
    for m in range(n_col):
        at = pl.ds(pl.multiple_of((col ^ m) * shard, shard), shard)
        kt[at, :] = kt_in[m][...]
        ujt[at, :] = ujt_in[m][...]
    zero = jnp.zeros((rank, rank), F32)
    kt[...] = jnp.where((sub < there) & (lane < here), kt[...].astype(F32), zero).astype(BF16)
    cl = jnp.where(lane < goal, nn(ujt[...], v_ref[...]), zero).astype(BF16)
    cu = jnp.where((sub < old) & (lane < goal), cu_ref[...], zero).astype(BF16).astype(F32)
    mf[pl.ds(0, rank), :] = cu
    mf[pl.ds(rank, rank), :] = -tn(kt[...], cl)
    hm[...] = nn(h_ref[...], mf[...], HIGHEST)
    g = tn(mf[...], hm[...], HIGHEST) + jnp.where(eye & (lane >= goal), 1.0, 0.0)
    dg = jnp.where(eye, g, 0.0)
    d_row = lax.rsqrt(jnp.sum(dg, axis=0, keepdims=True))
    d_col = lax.rsqrt(jnp.sum(dg, axis=1, keepdims=True))
    gn[...] = g * d_col * d_row
    scale = rank / jnp.sum(gn[...] * gn[...], keepdims=True)
    y_ref[...] = (one - lower_half(gn[...] * scale - one, eye, below)) * jnp.sqrt(scale)
    gb = gn[...].astype(BF16)

    def rough(carry):
        step, _ = carry
        y = y_ref[...]
        yb = y.astype(BF16)
        e = nt(nn(yb, gb).astype(BF16), yb) - one
        y_ref[...] = y - nn(lower_half(e, eye, below).astype(BF16), yb)
        return step + 1, jnp.max(jnp.abs(e))

    def fine(carry):
        step, _ = carry
        y = y_ref[...]
        e = nt(nn(y, gn[...], HIGHEST), y, HIGHEST) - one
        y_ref[...] = y - nn(lower_half(e, eye, below), y, HIGHEST)
        return step + 1, jnp.max(jnp.abs(e))

    lax.while_loop(lambda c: (c[0] < ROUGH_STEPS) & (c[1] > ROUGH), rough, (jnp.int32(0), F32(1.0)))
    _, err = lax.while_loop(lambda c: (c[0] < FINE_STEPS) & (c[1] > FINE), fine, (jnp.int32(0), F32(1.0)))

    lowest = jnp.min(jnp.where(eye, y_ref[...], 1.0))

    @pl.when(jnp.logical_not((err <= FINE) & (lowest > 0.0)))
    def _():
        a_ref[...] = gn[...]
        y_ref[...] = one

        def pivot(k, _):
            col = jnp.sum(jnp.where(lane == k, a_ref[...], 0.0), axis=1, keepdims=True)
            row = jnp.sum(jnp.where(sub == k, a_ref[...], 0.0), axis=0, keepdims=True)
            yrow = jnp.sum(jnp.where(sub == k, y_ref[...], 0.0), axis=0, keepdims=True)
            top = jnp.sum(jnp.where(lax.broadcasted_iota(jnp.int32, (1, rank), 1) == k, row, 0.0))
            inv = 1.0 / jnp.sqrt(jnp.full((1, rank), top))
            row, yrow = row * inv, yrow * inv
            col = jnp.where(lax.broadcasted_iota(jnp.int32, (rank, 1), 0) > k, col * inv[:, :1], 0.0)
            a_ref[...] = a_ref[...] - col * row
            y_ref[...] = jnp.where(sub == k, yrow, y_ref[...] - col * yrow)
            return 0

        lax.fori_loop(0, rank, pivot, 0)

    x = y_ref[...] * d_row
    root = math.sqrt(rows)
    c = nt(mf[...], x, HIGHEST) * root
    r = nt(hm[...], x, HIGHEST)
    r_up = jnp.where(sub < old, r[:rank], 0.0).astype(BF16)
    r_low = (-nn(kt[...].astype(F32), r[rank:], HIGHEST)).astype(BF16)
    ch, cl2 = halves(c)
    cu_h, cu_l, cl_h, cl_l = ch[:rank], cl2[:rank], ch[rank:], cl2[rank:]
    step = 256 if rows % 256 == 0 else rows
    for t in range(rows // step):
        at = pl.ds(t * step, step)
        u, v = u_ref[at, :], v_ref[at, :]
        ui, uj = uit_ref[:, at], ujt[:, at]
        q_ref[at, :] = (nn(u, cu_h) + nn(u, cu_l) + tn(ui, cl_h) + tn(ui, cl_l)).astype(BF16)
        w_ref[at, :] = (nn(v, r_up) + tn(uj, r_low)).astype(BF16)


def body(tile_basis, tile_coeffs, panel_basis, panel_coeffs, tile_rank, target_rank, panel_rank, owner_row):
    n_row, n_col = lax.axis_size("row"), lax.axis_size("col")
    u, v = tile_basis[0, 0], tile_coeffs[0, 0]
    pu, pv = panel_basis[0], panel_coeffs[0]
    rows, rank = u.shape

    parts = {}

    def left_parts():
        parts["left"] = xor_gather(pu, "col", n_col)
        return parts["left"]

    def right_parts():
        parts["right"] = xor_gather(after(pv, *parts["left"]), "col", n_col)
        return parts["right"]

    us, vs, rest = ring_gathers(pu, pv, "row", n_row, [left_parts, right_parts])
    ui_parts, vi_parts = parts["left"], parts["right"]
    uit, h, core_up = gram_products(u, v, ui_parts, n_col)
    rest((core_up,))

    ujs = picked_left(us, owner_row, n_row, n_col)
    ujs = [ujs[0]] + [swap(ujs[m], "col", n_col, m) for m in range(1, n_col)]
    kts = coupled(vs, vi_parts, owner_row, n_row, n_col)
    kts = [kts[0]] + [swap(kts[m], "col", n_col, m) for m in range(1, n_col)]

    out = jax.ShapeDtypeStruct((rows, rank), BF16)
    square = pltpu.VMEM((rank, rank), F32)
    fresh_basis, fresh_coeffs = pl.pallas_call(
        functools.partial(finish, n_col),
        out_shape=(out, out),
        in_specs=[SMEM] * 4 + [VMEM] * (5 + 2 * n_col),
        out_specs=(VMEM, VMEM),
        scratch_shapes=[
            pltpu.VMEM((rank, rows), BF16),
            pltpu.VMEM((rank, rank), BF16),
            pltpu.VMEM((2 * rank, rank), F32),
            pltpu.VMEM((2 * rank, rank), F32),
            square,
            square,
            square,
        ],
        compiler_params=pltpu.CompilerParams(vmem_limit_bytes=48 << 20),
        cost_estimate=pl.CostEstimate(flops=8 << 30, bytes_accessed=12 << 20, transcendentals=0),
        name="finish",
    )(tile_rank, target_rank, panel_rank, owner_row, u, v, uit, h, core_up, *ujs, *kts)
    return fresh_basis[None, None], fresh_coeffs[None, None]


def solution(mesh):
    tiles, panels = P("row", "col", None, None), P("row", "col", None)
    return jax.shard_map(
        body,
        mesh=mesh,
        in_specs=(tiles, tiles, panels, panels, P("row", "col"), P("row", "col"), P(), P()),
        out_specs=(tiles, tiles),
        check_vma=False,
    )
```

```python
import functools
import math

import jax
import jax.numpy as jnp
from jax import lax
from jax.experimental import pallas as pl
from jax.experimental.pallas import tpu as pltpu
from jax.sharding import PartitionSpec as P

F32 = jnp.float32
BF16 = jnp.bfloat16
HIGHEST = lax.Precision.HIGHEST
VMEM = pl.BlockSpec(memory_space=pltpu.VMEM)
SMEM = pl.BlockSpec(memory_space=pltpu.SMEM)
HBM = pl.BlockSpec(memory_space=pltpu.HBM)
ROUGH, FINE = 0.05, 0.015
ROUGH_STEPS, FINE_STEPS = 12, 6


def nn(a, b, precision=None):
    return lax.dot_general(a, b, (((1,), (0,)), ((), ())), precision=precision, preferred_element_type=F32)


def nt(a, b, precision=None):
    return lax.dot_general(a, b, (((1,), (1,)), ((), ())), precision=precision, preferred_element_type=F32)


def tn(a, b, precision=None):
    return lax.dot_general(a, b, (((0,), (0,)), ((), ())), precision=precision, preferred_element_type=F32)


def halves(x):
    high = x.astype(BF16)
    return high, (x - high.astype(F32)).astype(BF16)


def after(x, *others):
    return lax.optimization_barrier((x, *others))[0]


def ring_place(r, n):
    return jnp.where(r % 2 == 0, r // 2, n - 1 - r // 2)


def ring_steps(n):
    ring = list(range(0, n, 2)) + list(range(n - 1, 0, -2))
    ahead = [(ring[i], ring[(i + 1) % n]) for i in range(n)]
    return ahead, [(b, a) for a, b in ahead]


def farther(n_row, n_col, d):
    ring = [a for a, _ in ring_steps(n_row)[0]]
    pairs = []
    for at, r in enumerate(ring):
        for c in range(n_col):
            to = ring[(at + (d if c % 2 == 0 else -d)) % n_row]
            pairs.append((r * n_col + c, to * n_col + c))
    return pairs


def rings(left, right, n_row, n_col, gates):
    ahead, back = ring_steps(n_row)
    half = n_row // 2
    lefts, rights = [left] + [None] * (n_row - 1), [right]
    fwd = bwd = left
    step = lambda d: rights.append(lax.ppermute(rights[-1], ("row", "col"), farther(n_row, n_col, 1)))
    step(1)
    for s in range(1, half):
        if s > 1:
            lag = rights[s - 2 : s - 1] if s > 2 else ()
            fwd, bwd, *_ = lax.optimization_barrier((fwd, bwd, *lag, *(gates[s]() if s in gates else ())))
            step(s)
        fwd, bwd = lax.ppermute(fwd, "row", ahead), lax.ppermute(bwd, "row", back)
        lefts[s], lefts[n_row - s] = fwd, bwd
    gate = gates[half]() if half in gates else ()
    fwd, bwd, *_ = lax.optimization_barrier((fwd, bwd, rights[half - 2], *gate))
    low = left.shape[0] // 2
    lefts[half] = lax.ppermute(fwd[:low], "row", ahead)
    lefts.append(lax.ppermute(bwd[low:], "row", back))
    step(half)
    return lefts, rights


def swap(x, axis, n, m):
    return lax.ppermute(x, axis, [(i, i ^ m) for i in range(n)])


def part_copies(parts, target, sem):
    shard = target.shape[0] // len(parts)
    col = lax.axis_index("col")
    spots = [pl.ds(pl.multiple_of((col ^ m) * shard, shard), shard) for m in range(len(parts))]
    return [pltpu.make_async_copy(part, target.at[spots[m]], sem.at[m]) for m, part in enumerate(parts)]


def owner_steps(n_row, n_col, owner):
    row, col = lax.axis_index("row"), lax.axis_index("col")
    here = ring_place(row, n_row)
    return [lax.rem(here - ring_place(owner[col ^ m], n_row) + n_row, n_row) for m in range(n_col)]


def start_picks(pieces, n_row, steps, place, sems):
    low = pieces[0].shape[0] // 2

    def copy(m, k, h):
        if k == n_row // 2:
            source = pieces[n_row if h else k]
        else:
            source = pieces[k].at[pl.ds(h * low, low)]
        return pltpu.make_async_copy(source, place(m, h), sems[h].at[m])

    for m, step in enumerate(steps):
        for k in range(n_row):

            @pl.when(step == k)
            def _():
                copy(m, k, 0).start()
                copy(m, k, 1).start()

    return [copy(m, 0, h) for m in range(len(steps)) for h in range(2)]


def pick_left(n_row, n_col, owner, *refs):
    pieces, outs, sems = refs[: n_row + 1], refs[n_row + 1 : -2], refs[-2:]
    shard = pieces[0].shape[0]
    place = lambda m, h: outs[m].at[pl.ds(h * shard // 2, shard // 2)]
    for copy in start_picks(pieces, n_row, owner_steps(n_row, n_col, owner), place, sems):
        copy.wait()


def picked_left(pieces, owner, n_row, n_col):
    shard, width = pieces[0].shape
    return pl.pallas_call(
        functools.partial(pick_left, n_row, n_col),
        out_shape=[jax.ShapeDtypeStruct((shard, width), BF16)] * n_col,
        in_specs=[SMEM] + [HBM] * (n_row + 1),
        out_specs=[VMEM] * n_col,
        scratch_shapes=[pltpu.SemaphoreType.DMA((n_col,))] * 2,
        cost_estimate=pl.CostEstimate(flops=0, bytes_accessed=3 << 20, transcendentals=0),
        name="pick_left",
    )(owner, *pieces)


def couple(n_rights, *refs):
    rights, mates = refs[:n_rights], refs[n_rights : -n_rights - 4]
    outs = refs[-n_rights - 4 : -4]
    theirs, mine, sem, part_sem = refs[-4:]
    pair, half = rights[0].shape
    shard = pair // 2
    col = lax.axis_index("col")
    loads = [
        pltpu.make_async_copy(right, theirs.at[pl.ds(d * pair, pair)], sem.at[d]) for d, right in enumerate(rights)
    ]
    parts = []
    for m, mate in enumerate([rights[0], *mates]):
        for t in range(2):
            spot = pl.ds(pl.multiple_of((col ^ (2 * m) ^ t) * shard, shard), shard)
            parts.append(
                pltpu.make_async_copy(mate.at[pl.ds(t * shard, shard)], mine.at[spot], part_sem.at[2 * m + t])
            )
    for copy in [*loads, *parts]:
        copy.start()
    for copy in [*loads, *parts]:
        copy.wait()
    product = nt(theirs[...], mine[...]).astype(BF16)
    for d in range(n_rights):
        outs[d][...] = product[d * pair : (d + 1) * pair]


def coupled(rights, mates, n_col):
    pair, half = rights[0].shape
    rank = n_col * pair // 2
    count = len(rights)
    return pl.pallas_call(
        functools.partial(couple, count),
        out_shape=[jax.ShapeDtypeStruct((pair, rank), BF16)] * count,
        in_specs=[HBM] * (count + len(mates)),
        out_specs=[VMEM] * count,
        scratch_shapes=[
            pltpu.VMEM((count * pair, half), BF16),
            pltpu.VMEM((rank, half), BF16),
            pltpu.SemaphoreType.DMA((count,)),
            pltpu.SemaphoreType.DMA((n_col,)),
        ],
        compiler_params=pltpu.CompilerParams(vmem_limit_bytes=32 << 20),
        cost_estimate=pl.CostEstimate(
            flops=2 * count * pair * rank * half, bytes_accessed=3 << 20, transcendentals=0
        ),
        name="coupling",
    )(*rights, *mates)


def pick_products(n_row, n_col, owner, *refs):
    pieces, outs = refs[:n_row], refs[n_row:]
    odd = lax.rem(lax.axis_index("col"), 2) == 1
    for m, step in enumerate(owner_steps(n_row, n_col, owner)):
        at = jnp.where(odd, lax.rem(n_row - step, n_row), step)
        for k in range(n_row):

            @pl.when(at == k)
            def _():
                outs[m][...] = pieces[k][...]


def picked_products(pieces, owner, n_row, n_col):
    return pl.pallas_call(
        functools.partial(pick_products, n_row, n_col),
        out_shape=[jax.ShapeDtypeStruct(pieces[0].shape, BF16)] * n_col,
        in_specs=[SMEM] + [VMEM] * n_row,
        out_specs=[VMEM] * n_col,
        cost_estimate=pl.CostEstimate(flops=0, bytes_accessed=1 << 20, transcendentals=0),
        name="pick_products",
    )(owner, *pieces)


def grams(n_col, u_hbm, v_hbm, *refs):
    h_ref, cu_ref, u_ref, v_ref, uit, sem, part_sem = refs[n_col:]
    rank = cu_ref.shape[0]
    loads = [pltpu.make_async_copy(v_hbm, v_ref, sem.at[0]), pltpu.make_async_copy(u_hbm, u_ref, sem.at[1])]
    parts = part_copies(refs[:n_col], uit, part_sem)
    for copy in [*loads, *parts]:
        copy.start()
    top, bottom = pl.ds(0, rank), pl.ds(rank, rank)
    loads[0].wait()
    cu_ref[...] = tn(v_ref[...], v_ref[...])
    loads[1].wait()
    h_ref[top, :rank] = tn(u_ref[...], u_ref[...])
    for copy in parts:
        copy.wait()
    cross = nn(uit[...], u_ref[...])
    h_ref[bottom, :rank] = cross
    h_ref[top, rank:] = cross.T
    h_ref[bottom, rank:] = nt(uit[...], uit[...])


def gram_products(u, v, parts):
    rows, rank = u.shape
    tall = pltpu.VMEM((rows, rank), BF16)
    return pl.pallas_call(
        functools.partial(grams, len(parts)),
        out_shape=[jax.ShapeDtypeStruct((2 * rank, 2 * rank), F32), jax.ShapeDtypeStruct((rank, rank), F32)],
        in_specs=[HBM] * (2 + len(parts)),
        out_specs=[VMEM] * 2,
        scratch_shapes=[
            tall,
            tall,
            pltpu.VMEM((rank, rows), BF16),
            pltpu.SemaphoreType.DMA((2,)),
            pltpu.SemaphoreType.DMA((len(parts),)),
        ],
        compiler_params=pltpu.CompilerParams(vmem_limit_bytes=40 << 20),
        cost_estimate=pl.CostEstimate(flops=8 * rank * rank * rows, bytes_accessed=6 << 20, transcendentals=0),
        name="grams",
    )(u, v, *parts)


def lower_half(e, eye, below):
    return jnp.where(below, e, jnp.where(eye, 0.5 * e, 0.0))


def finish(n_row, n_col, old_ref, goal_ref, panel, owner, u_hbm, v_hbm, h_hbm, cu_hbm, *refs):
    ui_hbm, ujt_hbm, kt_in = refs[:n_col], refs[n_col : 2 * n_col], refs[2 * n_col : 3 * n_col]
    (q_hbm, w_hbm, u_ref, v_ref, uit_ref, h_ref, cu_ref, ujt, q_ref, w_ref, sides, kt, mf, hm, gn, y_ref, a_ref) = refs[
        3 * n_col : -5
    ]
    in_sem, ui_sem, uj_sem, q_sem, w_sem = refs[-5:]
    rows, rank = u_ref.shape
    shard = rank // n_col
    row, col = lax.axis_index("row"), lax.axis_index("col")
    loads = [
        pltpu.make_async_copy(src, dst, in_sem.at[t])
        for t, (src, dst) in enumerate(
            [(v_hbm, v_ref), (h_hbm, h_ref), (cu_hbm, cu_ref), (u_hbm, u_ref)]
        )
    ]
    ui_loads = part_copies(ui_hbm, uit_ref, ui_sem)
    uj_loads = part_copies(ujt_hbm, ujt, uj_sem)
    for copy in [*uj_loads, *loads, *ui_loads]:
        copy.start()
    old, goal, here, there = old_ref[0, 0], goal_ref[0, 0], panel[row], panel[owner[col]]
    sub = lax.broadcasted_iota(jnp.int32, (rank, rank), 0)
    lane = lax.broadcasted_iota(jnp.int32, (rank, rank), 1)
    eye, below = sub == lane, sub > lane
    one = jnp.where(eye, 1.0, 0.0).astype(F32)
    for m in range(n_col):
        other = col ^ m
        for t in range(2):
            spot = pl.ds(pl.multiple_of((other ^ t) * shard, shard), shard)
            sides[lax.rem(other, 2), spot, :] = kt_in[m][t * shard : (t + 1) * shard].astype(F32)
    step = owner_steps(n_row, 1, owner)[0]
    for side, at in enumerate((step, lax.rem(n_row - step, n_row))):

        @pl.when(at > n_row // 2)
        def _():
            sides[side] = sides[side].T

    zero = jnp.zeros((rank, rank), F32)
    kt[...] = jnp.where((sub < there) & (lane < here), sides[0] + sides[1], zero).astype(BF16)
    for copy in [*uj_loads, *loads[:1]]:
        copy.wait()
    cl = jnp.where(lane < goal, nn(ujt[...], v_ref[...]), zero).astype(BF16)
    for copy in loads[1:3]:
        copy.wait()
    cu = jnp.where((sub < old) & (lane < goal), cu_ref[...], zero).astype(BF16).astype(F32)
    mf[pl.ds(0, rank), :] = cu
    mf[pl.ds(rank, rank), :] = -tn(kt[...], cl)
    hm[...] = nn(h_ref[...], mf[...], HIGHEST)
    g = tn(mf[...], hm[...], HIGHEST) + jnp.where(eye & (lane >= goal), 1.0, 0.0)
    dg = jnp.where(eye, g, 0.0)
    d_row = lax.rsqrt(jnp.sum(dg, axis=0, keepdims=True))
    d_col = lax.rsqrt(jnp.sum(dg, axis=1, keepdims=True))
    gn[...] = g * d_col * d_row
    scale = rank / jnp.sum(gn[...] * gn[...], keepdims=True)
    y_ref[...] = (one - lower_half(gn[...] * scale - one, eye, below)) * jnp.sqrt(scale)
    gb = gn[...].astype(BF16)

    def rough(carry):
        step, _ = carry
        y = y_ref[...]
        yb = y.astype(BF16)
        e = nt(nn(yb, gb).astype(BF16), yb) - one
        y_ref[...] = y - nn(lower_half(e, eye, below).astype(BF16), yb)
        return step + 1, jnp.max(jnp.abs(e))

    def fine(carry):
        step, _ = carry
        y = y_ref[...]
        e = nt(nn(y, gn[...], HIGHEST), y, HIGHEST) - one
        y_ref[...] = y - nn(lower_half(e, eye, below), y, HIGHEST)
        return step + 1, jnp.max(jnp.abs(e))

    lax.while_loop(lambda c: (c[0] < ROUGH_STEPS) & (c[1] > ROUGH), rough, (jnp.int32(0), F32(1.0)))
    _, err = lax.while_loop(lambda c: (c[0] < FINE_STEPS) & (c[1] > FINE), fine, (jnp.int32(0), F32(1.0)))

    lowest = jnp.min(jnp.where(eye, y_ref[...], 1.0))

    @pl.when(jnp.logical_not((err <= FINE) & (lowest > 0.0)))
    def _():
        a_ref[...] = gn[...]
        y_ref[...] = one

        def pivot(k, _):
            col = jnp.sum(jnp.where(lane == k, a_ref[...], 0.0), axis=1, keepdims=True)
            row = jnp.sum(jnp.where(sub == k, a_ref[...], 0.0), axis=0, keepdims=True)
            yrow = jnp.sum(jnp.where(sub == k, y_ref[...], 0.0), axis=0, keepdims=True)
            top = jnp.sum(jnp.where(lax.broadcasted_iota(jnp.int32, (1, rank), 1) == k, row, 0.0))
            inv = 1.0 / jnp.sqrt(jnp.full((1, rank), top))
            row, yrow = row * inv, yrow * inv
            col = jnp.where(lax.broadcasted_iota(jnp.int32, (rank, 1), 0) > k, col * inv[:, :1], 0.0)
            a_ref[...] = a_ref[...] - col * row
            y_ref[...] = jnp.where(sub == k, yrow, y_ref[...] - col * yrow)
            return 0

        lax.fori_loop(0, rank, pivot, 0)

    x = y_ref[...] * d_row
    root = math.sqrt(rows)
    c = nt(mf[...], x, HIGHEST) * root
    r = nt(hm[...], x, HIGHEST)
    r_up = jnp.where(sub < old, r[:rank], 0.0).astype(BF16)
    r_low = (-nn(kt[...].astype(F32), r[rank:], HIGHEST)).astype(BF16)
    ch, cl2 = halves(c)
    cu_h, cu_l, cl_h, cl_l = ch[:rank], cl2[:rank], ch[rank:], cl2[rank:]
    for copy in [*loads[3:], *ui_loads]:
        copy.wait()
    step = rows // q_sem.shape[0]
    stores = []
    for t in range(rows // step):
        at = pl.ds(t * step, step)
        u, v = u_ref[at, :], v_ref[at, :]
        ui, uj = uit_ref[:, at], ujt[:, at]
        q_ref[at, :] = (nn(u, cu_h) + nn(u, cu_l) + tn(ui, cl_h) + tn(ui, cl_l)).astype(BF16)
        stores.append(pltpu.make_async_copy(q_ref.at[at], q_hbm.at[at], q_sem.at[t]))
        stores[-1].start()
        w_ref[at, :] = (nn(v, r_up) + tn(uj, r_low)).astype(BF16)
        stores.append(pltpu.make_async_copy(w_ref.at[at], w_hbm.at[at], w_sem.at[t]))
        stores[-1].start()
    for copy in stores:
        copy.wait()


def body(tile_basis, tile_coeffs, panel_basis, panel_coeffs, tile_rank, target_rank, panel_rank, owner_row):
    n_row, n_col = lax.axis_size("row"), lax.axis_size("col")
    u, v = tile_basis[0, 0], tile_coeffs[0, 0]
    pu, pv = panel_basis[0], panel_coeffs[0]
    rows, rank = u.shape

    odd = lax.axis_index("col") % 2
    cut = rows // 2
    own = lax.dynamic_slice_in_dim(pv, odd * cut, cut, 1)
    mate = swap(lax.dynamic_slice_in_dim(pv, (1 - odd) * cut, cut, 1), "col", n_col, 1)
    pair = jnp.concatenate([own, mate], 0)

    lefts, pairs = {0: pu}, {0: pair}

    def grow(have, gate, bits):
        for bit in bits:
            for m in list(have):
                have[m | bit] = swap(after(have[m], *gate), "col", n_col, bit)
        return tuple(have.values())

    high = [n_col >> t for t in range(1, n_col.bit_length() - 1)]
    half = n_row // 2
    gates = {half - 1: lambda: grow(lefts, (), high), half: lambda: grow(pairs, lefts.values(), high)}
    us, vs = rings(pu, pair, n_row, n_col, gates)
    grow(lefts, us[:3], [1])
    ui_parts = [lefts[m] for m in range(n_col)]

    ujs = picked_left(us, owner_row, n_row, n_col)
    ujs = [ujs[0]] + [swap(ujs[m], "col", n_col, m) for m in range(1, n_col)]
    near = coupled(vs, [pairs[m] for m in range(2, n_col, 2)], n_col)
    far = [lax.ppermute(near[d], ("row", "col"), farther(n_row, n_col, -d)) for d in range(half - 1, 0, -1)]
    kts = picked_products([*near, *far], owner_row, n_row, n_col)
    h, core_up = gram_products(u, v, [after(ui_parts[0], near[0]), *ui_parts[1:]])
    kts = [kts[0]] + [swap(kts[m], "col", n_col, m) for m in range(1, n_col)]

    out = jax.ShapeDtypeStruct((rows, rank), BF16)
    square = pltpu.VMEM((rank, rank), F32)
    tall, wide = pltpu.VMEM((rows, rank), BF16), pltpu.VMEM((rank, rows), BF16)
    tiles = rows // 256 if rows % 256 == 0 else 1
    fresh_basis, fresh_coeffs = pl.pallas_call(
        functools.partial(finish, n_row, n_col),
        out_shape=(out, out),
        in_specs=[SMEM] * 4 + [HBM] * (4 + 2 * n_col) + [VMEM] * n_col,
        out_specs=(HBM, HBM),
        scratch_shapes=[
            tall,
            tall,
            wide,
            pltpu.VMEM((2 * rank, 2 * rank), F32),
            square,
            wide,
            tall,
            tall,
            pltpu.VMEM((2, rank, rank), F32),
            pltpu.VMEM((rank, rank), BF16),
            pltpu.VMEM((2 * rank, rank), F32),
            pltpu.VMEM((2 * rank, rank), F32),
            square,
            square,
            square,
            pltpu.SemaphoreType.DMA((4,)),
            pltpu.SemaphoreType.DMA((n_col,)),
            pltpu.SemaphoreType.DMA((n_col,)),
            pltpu.SemaphoreType.DMA((tiles,)),
            pltpu.SemaphoreType.DMA((tiles,)),
        ],
        compiler_params=pltpu.CompilerParams(vmem_limit_bytes=40 << 20),
        cost_estimate=pl.CostEstimate(flops=8 << 30, bytes_accessed=12 << 20, transcendentals=0),
        name="finish",
    )(tile_rank, target_rank, panel_rank, owner_row, u, v, h, core_up, *ui_parts, *ujs, *kts)
    return fresh_basis[None, None], fresh_coeffs[None, None]


def solution(mesh):
    tiles, panels = P("row", "col", None, None), P("row", "col", None)
    return jax.shard_map(
        body,
        mesh=mesh,
        in_specs=(tiles, tiles, panels, panels, P("row", "col"), P("row", "col"), P(), P()),
        out_specs=(tiles, tiles),
        check_vma=False,
    )
```

```python
import functools
import math

import jax
import jax.numpy as jnp
from jax import lax
from jax.experimental import pallas as pl
from jax.experimental.pallas import tpu as pltpu
from jax.sharding import PartitionSpec as P

F32 = jnp.float32
BF16 = jnp.bfloat16
HIGHEST = lax.Precision.HIGHEST
VMEM = pl.BlockSpec(memory_space=pltpu.VMEM)
SMEM = pl.BlockSpec(memory_space=pltpu.SMEM)
HBM = pl.BlockSpec(memory_space=pltpu.HBM)
ROUGH, FINE = 0.05, 0.015
ROUGH_STEPS, FINE_STEPS = 12, 6


def nn(a, b, precision=None):
    return lax.dot_general(a, b, (((1,), (0,)), ((), ())), precision=precision, preferred_element_type=F32)


def nt(a, b, precision=None):
    return lax.dot_general(a, b, (((1,), (1,)), ((), ())), precision=precision, preferred_element_type=F32)


def tn(a, b, precision=None):
    return lax.dot_general(a, b, (((0,), (0,)), ((), ())), precision=precision, preferred_element_type=F32)


def halves(x):
    high = x.astype(BF16)
    return high, (x - high.astype(F32)).astype(BF16)


def after(x, *others):
    return lax.optimization_barrier((x, *others))[0]


def ring_place(r, n):
    return jnp.where(r % 2 == 0, r // 2, n - 1 - r // 2)


def ring_steps(n):
    ring = list(range(0, n, 2)) + list(range(n - 1, 0, -2))
    ahead = [(ring[i], ring[(i + 1) % n]) for i in range(n)]
    return ahead, [(b, a) for a, b in ahead]


def ring_gathers(left, right, axis, n, gates):
    ahead, back = ring_steps(n)
    half, low = n // 2, left.shape[0] // 2
    lists = [[panel] + [None] * (n - 1) for panel in (left, right)]
    now = [(left, left), (right, right)]

    def step(panel, s, *gate):
        fwd, bwd, *_ = lax.optimization_barrier((*now[panel], *gate))
        if s == half:
            fwd, bwd = fwd[:low], bwd[low:]
        fwd, bwd = lax.ppermute(fwd, axis, ahead), lax.ppermute(bwd, axis, back)
        now[panel] = fwd, bwd
        if s == half:
            lists[panel][half] = fwd
            lists[panel].append(bwd)
        else:
            lists[panel][s], lists[panel][n - s] = fwd, bwd
        return fwd, bwd

    for s in range(1, half - 1):
        done = step(0, s)
    for s in range(1, half + 1):
        if s < 3:
            early = step(0, half - 2 + s)
        gate = gates[s](lists) if s in gates else ()
        step(1, s, *gate, *(done if s < 3 else ()))
        done = early
    return lists


def swap(x, axis, n, m):
    return lax.ppermute(x, axis, [(i, i ^ m) for i in range(n)])


def part_copies(parts, target, sem):
    shard = target.shape[0] // len(parts)
    col = lax.axis_index("col")
    spots = [pl.ds(pl.multiple_of((col ^ m) * shard, shard), shard) for m in range(len(parts))]
    return [pltpu.make_async_copy(part, target.at[spots[m]], sem.at[m]) for m, part in enumerate(parts)]


def owner_steps(n_row, n_col, owner):
    row, col = lax.axis_index("row"), lax.axis_index("col")
    here = ring_place(row, n_row)
    return [lax.rem(here - ring_place(owner[col ^ m], n_row) + n_row, n_row) for m in range(n_col)]


def pick(pieces, n_row, n_col, owner, outs):
    low = pieces[0].shape[0] // 2
    for m, step in enumerate(owner_steps(n_row, n_col, owner)):
        for k in range(n_row):

            @pl.when(step == k)
            def _():
                if k == n_row // 2:
                    outs[m][:low] = pieces[k][...]
                    outs[m][low:] = pieces[n_row][...]
                else:
                    outs[m][...] = pieces[k][...]


def pick_left(n_row, n_col, owner, *refs):
    pick(refs[: n_row + 1], n_row, n_col, owner, refs[n_row + 1 :])


def picked_left(pieces, owner, n_row, n_col):
    shard, width = pieces[0].shape
    return pl.pallas_call(
        functools.partial(pick_left, n_row, n_col),
        out_shape=[jax.ShapeDtypeStruct((shard, width), BF16)] * n_col,
        in_specs=[SMEM] + [VMEM] * (n_row + 1),
        out_specs=[VMEM] * n_col,
        cost_estimate=pl.CostEstimate(flops=0, bytes_accessed=3 << 20, transcendentals=0),
        name="pick_left",
    )(owner, *pieces)


def couple(n_row, n_col, owner, *refs):
    pieces, parts = refs[: n_row + 1], refs[n_row + 1 : n_row + 1 + n_col]
    outs = refs[n_row + 1 + n_col : n_row + 1 + 2 * n_col]
    picked, mine = refs[n_row + 1 + 2 * n_col :]
    shard = pieces[0].shape[0]
    col = lax.axis_index("col")
    for m in range(n_col):
        mine[pl.ds(pl.multiple_of((col ^ m) * shard, shard), shard), :] = parts[m][...]
    pick(pieces, n_row, n_col, owner, [picked.at[pl.ds(m * shard, shard)] for m in range(n_col)])
    product = nt(picked[...], mine[...]).astype(BF16)
    for m in range(n_col):
        outs[m][...] = product[m * shard : (m + 1) * shard]


def coupled(pieces, parts, owner, n_row, n_col):
    shard, width = pieces[0].shape
    rank = n_col * shard
    return pl.pallas_call(
        functools.partial(couple, n_row, n_col),
        out_shape=[jax.ShapeDtypeStruct((shard, rank), BF16)] * n_col,
        in_specs=[SMEM] + [VMEM] * (n_row + 1 + n_col),
        out_specs=[VMEM] * n_col,
        scratch_shapes=[pltpu.VMEM((rank, width), BF16), pltpu.VMEM((rank, width), BF16)],
        compiler_params=pltpu.CompilerParams(vmem_limit_bytes=32 << 20),
        cost_estimate=pl.CostEstimate(flops=2 * rank * rank * width, bytes_accessed=3 << 20, transcendentals=0),
        name="coupling",
    )(owner, *pieces, *parts)


def grams(n_col, u_hbm, v_hbm, *refs):
    high, low, cu_ref, u_ref, v_ref, uit, sem, part_sem = refs[n_col:]
    rank = cu_ref.shape[0]
    loads = [pltpu.make_async_copy(v_hbm, v_ref, sem.at[0]), pltpu.make_async_copy(u_hbm, u_ref, sem.at[1])]
    parts = part_copies(refs[:n_col], uit, part_sem)
    for copy in [*loads, *parts]:
        copy.start()
    top, bottom = pl.ds(0, rank), pl.ds(rank, rank)

    def put(at, lanes, value):
        high[at, lanes], low[at, lanes] = halves(value)

    loads[0].wait()
    cu_ref[...] = tn(v_ref[...], v_ref[...])
    loads[1].wait()
    put(top, top, tn(u_ref[...], u_ref[...]))
    for copy in parts:
        copy.wait()
    cross = nn(uit[...], u_ref[...])
    put(bottom, top, cross)
    put(top, bottom, cross.T)
    put(bottom, bottom, nt(uit[...], uit[...]))


def gram_products(u, v, parts):
    rows, rank = u.shape
    tall = pltpu.VMEM((rows, rank), BF16)
    return pl.pallas_call(
        functools.partial(grams, len(parts)),
        out_shape=[jax.ShapeDtypeStruct((2 * rank, 2 * rank), BF16)] * 2 + [jax.ShapeDtypeStruct((rank, rank), F32)],
        in_specs=[HBM] * (2 + len(parts)),
        out_specs=[VMEM] * 3,
        scratch_shapes=[
            tall,
            tall,
            pltpu.VMEM((rank, rows), BF16),
            pltpu.SemaphoreType.DMA((2,)),
            pltpu.SemaphoreType.DMA((len(parts),)),
        ],
        compiler_params=pltpu.CompilerParams(vmem_limit_bytes=40 << 20),
        cost_estimate=pl.CostEstimate(flops=8 * rank * rank * rows, bytes_accessed=6 << 20, transcendentals=0),
        name="grams",
    )(u, v, *parts)


def lower_half(e, eye, below):
    return jnp.where(below, e, jnp.where(eye, 0.5 * e, 0.0))


def finish(n_col, old_ref, goal_ref, panel, owner, u_hbm, v_hbm, hh_hbm, hl_hbm, cu_hbm, *refs):
    ui_hbm, ujt_hbm, kt_in = refs[:n_col], refs[n_col : 2 * n_col], refs[2 * n_col : 3 * n_col]
    (q_hbm, w_hbm, u_ref, v_ref, uit_ref, hh, hl, cu_ref, ujt, q_ref, w_ref, kt, mh, gn, y_ref, a_ref) = refs[
        3 * n_col : -5
    ]
    in_sem, ui_sem, uj_sem, q_sem, w_sem = refs[-5:]
    rows, rank = u_ref.shape
    shard = rank // n_col
    row, col = lax.axis_index("row"), lax.axis_index("col")
    spots = [pl.ds(pl.multiple_of((col ^ m) * shard, shard), shard) for m in range(n_col)]
    loads = [
        pltpu.make_async_copy(src, dst, in_sem.at[t])
        for t, (src, dst) in enumerate(
            [(v_hbm, v_ref), (hh_hbm, hh), (hl_hbm, hl), (cu_hbm, cu_ref), (u_hbm, u_ref)]
        )
    ]
    ui_loads = part_copies(ui_hbm, uit_ref, ui_sem)
    uj_loads = [pltpu.make_async_copy(ujt_hbm[m], ujt.at[spots[m]], uj_sem.at[m]) for m in range(n_col)]
    for copy in [*uj_loads, *loads, *ui_loads]:
        copy.start()
    old, goal, here, there = old_ref[0, 0], goal_ref[0, 0], panel[row], panel[owner[col]]
    sub = lax.broadcasted_iota(jnp.int32, (rank, rank), 0)
    lane = lax.broadcasted_iota(jnp.int32, (rank, rank), 1)
    eye, below = sub == lane, sub > lane
    one = jnp.where(eye, 1.0, 0.0).astype(F32)
    for m in range(n_col):
        kt[spots[m], :] = kt_in[m][...]
    zero = jnp.zeros((rank, rank), F32)
    kt[...] = jnp.where((sub < there) & (lane < here), kt[...].astype(F32), zero).astype(BF16)
    for copy in [*uj_loads, *loads[:1]]:
        copy.wait()
    cl = jnp.where(lane < goal, nn(ujt[...], v_ref[...]), zero).astype(BF16)
    for copy in loads[1:4]:
        copy.wait()
    cu = jnp.where((sub < old) & (lane < goal), cu_ref[...], zero).astype(BF16)
    m_high, m_low = halves(-tn(kt[...], cl))
    mh[pl.ds(0, rank), :], mh[pl.ds(rank, rank), :] = cu, m_high
    hm = nn(hh[...], mh[...]) + nn(hl[...], mh[...]) + nn(hh[:, rank:], m_low)
    hm_high, hm_low = halves(hm)
    g = tn(mh[...], hm_high) + tn(mh[...], hm_low) + tn(m_low, hm_high[rank:])
    g = g + jnp.where(eye & (lane >= goal), 1.0, 0.0)
    dg = jnp.where(eye, g, 0.0)
    d_row = lax.rsqrt(jnp.sum(dg, axis=0, keepdims=True))
    d_col = lax.rsqrt(jnp.sum(dg, axis=1, keepdims=True))
    g = g * d_col * d_row
    gn[...] = g
    scale = rank / jnp.sum(g * g, keepdims=True)
    a_ref[...] = g * scale
    y_ref[...] = one * jnp.sqrt(scale)

    def rough(carry):
        step, _ = carry
        a = a_ref[...]
        e = a - one
        f = lower_half(e, eye, below).astype(BF16)
        y = y_ref[...]
        t = a - nn(f, a.astype(BF16))
        y_ref[...] = y - nn(f, y.astype(BF16))
        a_ref[...] = t - nt(t.astype(BF16), f)
        return step + 1, jnp.max(jnp.abs(e))

    def fine(carry):
        step, _ = carry
        y = y_ref[...]
        yh, yl = halves(y)
        gh, gl = halves(gn[...])
        th, tl = halves(nn(yh, gh) + nn(yh, gl) + nn(yl, gh))
        e = nt(th, yh) + nt(th, yl) + nt(tl, yh) - one
        y_ref[...] = y - nn(lower_half(e, eye, below).astype(BF16), yh)
        return step + 1, jnp.max(jnp.abs(e))

    lax.while_loop(lambda c: (c[0] < ROUGH_STEPS) & (c[1] > ROUGH), rough, (jnp.int32(0), F32(1.0)))
    _, err = lax.while_loop(lambda c: (c[0] < FINE_STEPS) & (c[1] > FINE), fine, (jnp.int32(0), F32(1.0)))
    lowest = jnp.min(jnp.where(eye, y_ref[...], 1.0))

    @pl.when(jnp.logical_not((err <= FINE) & (lowest > 0.0)))
    def _():
        a_ref[...] = gn[...]
        y_ref[...] = one

        def pivot(k, _):
            col = jnp.sum(jnp.where(lane == k, a_ref[...], 0.0), axis=1, keepdims=True)
            row = jnp.sum(jnp.where(sub == k, a_ref[...], 0.0), axis=0, keepdims=True)
            yrow = jnp.sum(jnp.where(sub == k, y_ref[...], 0.0), axis=0, keepdims=True)
            top = jnp.sum(jnp.where(lax.broadcasted_iota(jnp.int32, (1, rank), 1) == k, row, 0.0))
            inv = 1.0 / jnp.sqrt(jnp.full((1, rank), top))
            row, yrow = row * inv, yrow * inv
            col = jnp.where(lax.broadcasted_iota(jnp.int32, (rank, 1), 0) > k, col * inv[:, :1], 0.0)
            a_ref[...] = a_ref[...] - col * row
            y_ref[...] = jnp.where(sub == k, yrow, y_ref[...] - col * yrow)
            return 0

        lax.fori_loop(0, rank, pivot, 0)

    xh, xl = halves(y_ref[...] * d_row)
    root = math.sqrt(rows)
    c = nt(mh[...], xh) + nt(mh[...], xl)
    c_up = (c[:rank] * root).astype(BF16)
    c_low = ((c[rank:] + nt(m_low, xh)) * root).astype(BF16)
    r = nt(hm_high, xh) + nt(hm_high, xl) + nt(hm_low, xh)
    r_up = jnp.where(sub < old, r[:rank], 0.0).astype(BF16)
    w_high, w_low = halves(r[rank:])
    r_low = (-(nn(kt[...], w_high) + nn(kt[...], w_low))).astype(BF16)
    for copy in [*loads[4:], *ui_loads]:
        copy.wait()
    step = rows // q_sem.shape[0]
    stores = []
    for t in range(rows // step):
        at = pl.ds(t * step, step)
        u, v = u_ref[at, :], v_ref[at, :]
        ui, uj = uit_ref[:, at], ujt[:, at]
        q_ref[at, :] = (nn(u, c_up) + tn(ui, c_low)).astype(BF16)
        stores.append(pltpu.make_async_copy(q_ref.at[at], q_hbm.at[at], q_sem.at[t]))
        stores[-1].start()
        w_ref[at, :] = (nn(v, r_up) + tn(uj, r_low)).astype(BF16)
        stores.append(pltpu.make_async_copy(w_ref.at[at], w_hbm.at[at], w_sem.at[t]))
        stores[-1].start()
    for copy in stores:
        copy.wait()


def body(tile_basis, tile_coeffs, panel_basis, panel_coeffs, tile_rank, target_rank, panel_rank, owner_row):
    n_row, n_col = lax.axis_size("row"), lax.axis_size("col")
    u, v = tile_basis[0, 0], tile_coeffs[0, 0]
    pu, pv = panel_basis[0], panel_coeffs[0]
    rows, rank = u.shape

    lefts, rights, grammed = {0: pu}, {0: pv}, []

    def grow(have, bits):
        for bit in bits:
            for m in list(have):
                have[m | bit] = swap(have[m], "col", n_col, bit)
        return tuple(have.values())

    high = [n_col >> t for t in range(1, n_col.bit_length() - 1)]

    def columns_grams(lists):
        grow(lefts, [1])
        grow(rights, [1])
        grammed.extend(gram_products(u, v, [lefts[m] for m in range(n_col)]))
        return (grammed[2], *rights.values())

    gates = {1: lambda _: grow(lefts, high) + grow(rights, high), n_row // 2: columns_grams}
    us, vs = ring_gathers(pu, pv, "row", n_row, gates)
    h_high, h_low, core_up = grammed
    ui_parts = [lefts[m] for m in range(n_col)]

    ujs = picked_left(us, owner_row, n_row, n_col)
    ujs = [ujs[0]] + [swap(ujs[m], "col", n_col, m) for m in range(1, n_col)]
    kts = coupled(vs, [rights[m] for m in range(n_col)], owner_row, n_row, n_col)
    kts = [kts[0]] + [swap(kts[m], "col", n_col, m) for m in range(1, n_col)]

    out = jax.ShapeDtypeStruct((rows, rank), BF16)
    square = pltpu.VMEM((rank, rank), F32)
    tall, wide = pltpu.VMEM((rows, rank), BF16), pltpu.VMEM((rank, rows), BF16)
    tiles = rows // 256 if rows % 256 == 0 else 1
    fresh_basis, fresh_coeffs = pl.pallas_call(
        functools.partial(finish, n_col),
        out_shape=(out, out),
        in_specs=[SMEM] * 4 + [HBM] * (5 + 2 * n_col) + [VMEM] * n_col,
        out_specs=(HBM, HBM),
        scratch_shapes=[
            tall,
            tall,
            wide,
            pltpu.VMEM((2 * rank, 2 * rank), BF16),
            pltpu.VMEM((2 * rank, 2 * rank), BF16),
            square,
            wide,
            tall,
            tall,
            pltpu.VMEM((rank, rank), BF16),
            pltpu.VMEM((2 * rank, rank), BF16),
            square,
            square,
            square,
            pltpu.SemaphoreType.DMA((5,)),
            pltpu.SemaphoreType.DMA((n_col,)),
            pltpu.SemaphoreType.DMA((n_col,)),
            pltpu.SemaphoreType.DMA((tiles,)),
            pltpu.SemaphoreType.DMA((tiles,)),
        ],
        compiler_params=pltpu.CompilerParams(vmem_limit_bytes=40 << 20),
        cost_estimate=pl.CostEstimate(flops=8 << 30, bytes_accessed=12 << 20, transcendentals=0),
        name="finish",
    )(tile_rank, target_rank, panel_rank, owner_row, u, v, h_high, h_low, core_up, *ui_parts, *ujs, *kts)
    return fresh_basis[None, None], fresh_coeffs[None, None]


def solution(mesh):
    tiles, panels = P("row", "col", None, None), P("row", "col", None)
    return jax.shard_map(
        body,
        mesh=mesh,
        in_specs=(tiles, tiles, panels, panels, P("row", "col"), P("row", "col"), P(), P()),
        out_specs=(tiles, tiles),
        check_vma=False,
    )
```

```python
import functools
import math

import jax
import jax.numpy as jnp
from jax import lax
from jax.experimental import pallas as pl
from jax.experimental.pallas import tpu as pltpu
from jax.sharding import PartitionSpec as P

F32 = jnp.float32
BF16 = jnp.bfloat16
VMEM = pl.BlockSpec(memory_space=pltpu.VMEM)
SMEM = pl.BlockSpec(memory_space=pltpu.SMEM)
HBM = pl.BlockSpec(memory_space=pltpu.HBM)
ROUGH, FINE = 0.05, 0.015
ROUGH_STEPS, FINE_STEPS = 12, 6


def nn(a, b):
    return lax.dot_general(a, b, (((1,), (0,)), ((), ())), preferred_element_type=F32)


def nt(a, b):
    return lax.dot_general(a, b, (((1,), (1,)), ((), ())), preferred_element_type=F32)


def tn(a, b):
    return lax.dot_general(a, b, (((0,), (0,)), ((), ())), preferred_element_type=F32)


def halves(x):
    high = x.astype(BF16)
    return high, (x - high.astype(F32)).astype(BF16)


def after(x, *others):
    return lax.optimization_barrier((x, *others))[0]


def ring_place(r, n):
    return jnp.where(r % 2 == 0, r // 2, n - 1 - r // 2)


def ring_steps(n):
    ring = list(range(0, n, 2)) + list(range(n - 1, 0, -2))
    ahead = [(ring[i], ring[(i + 1) % n]) for i in range(n)]
    return ahead, [(b, a) for a, b in ahead]


def ring_gathers(left, right, axis, n, gates):
    ahead, back = ring_steps(n)
    half, low = n // 2, left.shape[0] // 2
    lists = [[panel] + [None] * (n - 1) for panel in (left, right)]
    now = [(left, left), (right, right)]

    def step(panel, s, *gate):
        fwd, bwd, *_ = lax.optimization_barrier((*now[panel], *gate))
        if s == half:
            fwd, bwd = fwd[:low], bwd[low:]
        fwd, bwd = lax.ppermute(fwd, axis, ahead), lax.ppermute(bwd, axis, back)
        now[panel] = fwd, bwd
        if s == half:
            lists[panel][half] = fwd
            lists[panel].append(bwd)
        else:
            lists[panel][s], lists[panel][n - s] = fwd, bwd
        return fwd, bwd

    for s in range(1, half - 1):
        done = step(0, s, *(gates[0](s) if s > 1 else ()))
    for s in range(1, half + 1):
        if s < 3:
            early = step(0, half - 2 + s)
        gate = gates[s](lists) if s in gates else ()
        step(1, s, *gate, *(done if s < 3 else ()))
        done = early
    return lists


def swap(x, axis, n, m):
    return lax.ppermute(x, axis, [(i, i ^ m) for i in range(n)])


def part_copies(parts, target, sem):
    shard = target.shape[0] // len(parts)
    col = lax.axis_index("col")
    spots = [pl.ds(pl.multiple_of((col ^ m) * shard, shard), shard) for m in range(len(parts))]
    return [pltpu.make_async_copy(part, target.at[spots[m]], sem.at[m]) for m, part in enumerate(parts)]


def owner_steps(n_row, n_col, owner):
    row, col = lax.axis_index("row"), lax.axis_index("col")
    here = ring_place(row, n_row)
    return [lax.rem(here - ring_place(owner[col ^ m], n_row) + n_row, n_row) for m in range(n_col)]


def pick(pieces, n_row, n_col, owner, outs):
    low = pieces[0].shape[0] // 2
    for m, step in enumerate(owner_steps(n_row, n_col, owner)):
        for k in range(n_row):

            @pl.when(step == k)
            def _():
                if k == n_row // 2:
                    outs[m][:low] = pieces[k][...]
                    outs[m][low:] = pieces[n_row][...]
                else:
                    outs[m][...] = pieces[k][...]


def pick_left(n_row, n_col, owner, *refs):
    pick(refs[: n_row + 1], n_row, n_col, owner, refs[n_row + 1 :])


def picked_left(pieces, owner, n_row, n_col):
    shard, width = pieces[0].shape
    return pl.pallas_call(
        functools.partial(pick_left, n_row, n_col),
        out_shape=[jax.ShapeDtypeStruct((shard, width), BF16)] * n_col,
        in_specs=[SMEM] + [VMEM] * (n_row + 1),
        out_specs=[VMEM] * n_col,
        cost_estimate=pl.CostEstimate(flops=0, bytes_accessed=3 << 20, transcendentals=0),
        name="pick_left",
    )(owner, *pieces)


def couple(n_row, n_col, owner, *refs):
    pieces, parts = refs[: n_row + 1], refs[n_row + 1 : n_row + 1 + n_col]
    outs = refs[n_row + 1 + n_col : n_row + 1 + 2 * n_col]
    picked, mine = refs[n_row + 1 + 2 * n_col :]
    shard = pieces[0].shape[0]
    col = lax.axis_index("col")
    for m in range(n_col):
        mine[pl.ds(pl.multiple_of((col ^ m) * shard, shard), shard), :] = parts[m][...]
    pick(pieces, n_row, n_col, owner, [picked.at[pl.ds(m * shard, shard)] for m in range(n_col)])
    product = nt(picked[...], mine[...]).astype(BF16)
    for m in range(n_col):
        outs[m][...] = product[m * shard : (m + 1) * shard]


def coupled(pieces, parts, owner, n_row, n_col):
    shard, width = pieces[0].shape
    rank = n_col * shard
    return pl.pallas_call(
        functools.partial(couple, n_row, n_col),
        out_shape=[jax.ShapeDtypeStruct((shard, rank), BF16)] * n_col,
        in_specs=[SMEM] + [VMEM] * (n_row + 1 + n_col),
        out_specs=[VMEM] * n_col,
        scratch_shapes=[pltpu.VMEM((rank, width), BF16), pltpu.VMEM((rank, width), BF16)],
        compiler_params=pltpu.CompilerParams(vmem_limit_bytes=32 << 20),
        cost_estimate=pl.CostEstimate(flops=2 * rank * rank * width, bytes_accessed=3 << 20, transcendentals=0),
        name="coupling",
    )(owner, *pieces, *parts)


def grams(n_col, u_hbm, v_hbm, *refs):
    high, low, cu_ref, u_ref, v_ref, uit, sem, part_sem = refs[n_col:]
    rank = cu_ref.shape[0]
    loads = [pltpu.make_async_copy(v_hbm, v_ref, sem.at[0]), pltpu.make_async_copy(u_hbm, u_ref, sem.at[1])]
    parts = part_copies(refs[:n_col], uit, part_sem)
    for copy in [*loads, *parts]:
        copy.start()
    top, bottom = pl.ds(0, rank), pl.ds(rank, rank)

    def put(at, lanes, value):
        high[at, lanes], low[at, lanes] = halves(value)

    loads[0].wait()
    cu_ref[...] = tn(v_ref[...], v_ref[...])
    loads[1].wait()
    put(top, top, tn(u_ref[...], u_ref[...]))
    for copy in parts:
        copy.wait()
    cross = nn(uit[...], u_ref[...])
    put(bottom, top, cross)
    put(top, bottom, cross.T)
    put(bottom, bottom, nt(uit[...], uit[...]))


def gram_products(u, v, parts):
    rows, rank = u.shape
    tall = pltpu.VMEM((rows, rank), BF16)
    return pl.pallas_call(
        functools.partial(grams, len(parts)),
        out_shape=[jax.ShapeDtypeStruct((2 * rank, 2 * rank), BF16)] * 2 + [jax.ShapeDtypeStruct((rank, rank), F32)],
        in_specs=[HBM] * (2 + len(parts)),
        out_specs=[VMEM] * 3,
        scratch_shapes=[
            tall,
            tall,
            pltpu.VMEM((rank, rows), BF16),
            pltpu.SemaphoreType.DMA((2,)),
            pltpu.SemaphoreType.DMA((len(parts),)),
        ],
        compiler_params=pltpu.CompilerParams(vmem_limit_bytes=40 << 20),
        cost_estimate=pl.CostEstimate(flops=8 * rank * rank * rows, bytes_accessed=6 << 20, transcendentals=0),
        name="grams",
    )(u, v, *parts)


def lower_half(e, eye, below):
    return jnp.where(below, e, jnp.where(eye, 0.5 * e, 0.0))


def finish(n_col, old_ref, goal_ref, panel, owner, u_hbm, v_hbm, hh_hbm, hl_hbm, cu_hbm, *refs):
    ui_hbm, ujt_hbm, kt_in = refs[:n_col], refs[n_col : 2 * n_col], refs[2 * n_col : 3 * n_col]
    (q_hbm, w_hbm, u_ref, v_ref, uit_ref, hh, hl, cu_ref, ujt, q_ref, w_ref, kt, mh, gn, y_ref, a_ref) = refs[
        3 * n_col : -5
    ]
    in_sem, ui_sem, uj_sem, q_sem, w_sem = refs[-5:]
    rows, rank = u_ref.shape
    shard = rank // n_col
    row, col = lax.axis_index("row"), lax.axis_index("col")
    spots = [pl.ds(pl.multiple_of((col ^ m) * shard, shard), shard) for m in range(n_col)]
    loads = [
        pltpu.make_async_copy(src, dst, in_sem.at[t])
        for t, (src, dst) in enumerate(
            [(v_hbm, v_ref), (hh_hbm, hh), (hl_hbm, hl), (cu_hbm, cu_ref), (u_hbm, u_ref)]
        )
    ]
    ui_loads = part_copies(ui_hbm, uit_ref, ui_sem)
    uj_loads = [pltpu.make_async_copy(ujt_hbm[m], ujt.at[spots[m]], uj_sem.at[m]) for m in range(n_col)]
    for copy in [*uj_loads, *loads, *ui_loads]:
        copy.start()
    old, goal, here, there = old_ref[0, 0], goal_ref[0, 0], panel[row], panel[owner[col]]
    sub = lax.broadcasted_iota(jnp.int32, (rank, rank), 0)
    lane = lax.broadcasted_iota(jnp.int32, (rank, rank), 1)
    eye, below = sub == lane, sub > lane
    one = jnp.where(eye, 1.0, 0.0).astype(F32)
    for m in range(n_col):
        kt[spots[m], :] = kt_in[m][...]
    zero = jnp.zeros((rank, rank), F32)
    kt[...] = jnp.where((sub < there) & (lane < here), kt[...].astype(F32), zero).astype(BF16)
    for copy in [*uj_loads, *loads[:1]]:
        copy.wait()
    cl = jnp.where(lane < goal, nn(ujt[...], v_ref[...]), zero).astype(BF16)
    for copy in loads[1:4]:
        copy.wait()
    cu = jnp.where((sub < old) & (lane < goal), cu_ref[...], zero).astype(BF16)
    m_high, m_low = halves(-tn(kt[...], cl))
    mh[pl.ds(0, rank), :], mh[pl.ds(rank, rank), :] = cu, m_high
    hm = nn(hh[...], mh[...]) + nn(hl[...], mh[...]) + nn(hh[:, rank:], m_low)
    hm_high, hm_low = halves(hm)
    g = tn(mh[...], hm_high) + tn(mh[...], hm_low) + tn(m_low, hm_high[rank:])
    g = g + jnp.where(eye & (lane >= goal), 1.0, 0.0)
    dg = jnp.where(eye, g, 0.0)
    d_row = lax.rsqrt(jnp.sum(dg, axis=0, keepdims=True))
    d_col = lax.rsqrt(jnp.sum(dg, axis=1, keepdims=True))
    g = g * d_col * d_row
    gn[...] = g
    scale = rank / jnp.sum(g * g, keepdims=True)
    a_ref[...] = g * scale
    y_ref[...] = one * jnp.sqrt(scale)

    def rough(carry):
        step, _ = carry
        a = a_ref[...]
        e = a - one
        f = lower_half(e, eye, below).astype(BF16)
        y = y_ref[...]
        t = a - nn(f, a.astype(BF16))
        y_ref[...] = y - nn(f, y.astype(BF16))
        a_ref[...] = t - nt(t.astype(BF16), f)
        return step + 1, jnp.max(jnp.abs(e))

    def fine(carry):
        step, _ = carry
        y = y_ref[...]
        yh, yl = halves(y)
        gh, gl = halves(gn[...])
        th, tl = halves(nn(yh, gh) + nn(yh, gl) + nn(yl, gh))
        e = nt(th, yh) + nt(th, yl) + nt(tl, yh) - one
        y_ref[...] = y - nn(lower_half(e, eye, below).astype(BF16), yh)
        return step + 1, jnp.max(jnp.abs(e))

    lax.while_loop(lambda c: (c[0] < ROUGH_STEPS) & (c[1] > ROUGH), rough, (jnp.int32(0), F32(1.0)))
    _, err = lax.while_loop(lambda c: (c[0] < FINE_STEPS) & (c[1] > FINE), fine, (jnp.int32(0), F32(1.0)))
    lowest = jnp.min(jnp.where(eye, y_ref[...], 1.0))

    @pl.when(jnp.logical_not((err <= FINE) & (lowest > 0.0)))
    def _():
        a_ref[...] = gn[...]
        y_ref[...] = one

        def pivot(k, _):
            col = jnp.sum(jnp.where(lane == k, a_ref[...], 0.0), axis=1, keepdims=True)
            row = jnp.sum(jnp.where(sub == k, a_ref[...], 0.0), axis=0, keepdims=True)
            yrow = jnp.sum(jnp.where(sub == k, y_ref[...], 0.0), axis=0, keepdims=True)
            top = jnp.sum(jnp.where(lax.broadcasted_iota(jnp.int32, (1, rank), 1) == k, row, 0.0))
            inv = 1.0 / jnp.sqrt(jnp.full((1, rank), top))
            row, yrow = row * inv, yrow * inv
            col = jnp.where(lax.broadcasted_iota(jnp.int32, (rank, 1), 0) > k, col * inv[:, :1], 0.0)
            a_ref[...] = a_ref[...] - col * row
            y_ref[...] = jnp.where(sub == k, yrow, y_ref[...] - col * yrow)
            return 0

        lax.fori_loop(0, rank, pivot, 0)

    xh, xl = halves(y_ref[...] * d_row)
    root = math.sqrt(rows)
    c = nt(mh[...], xh) + nt(mh[...], xl)
    c_up = (c[:rank] * root).astype(BF16)
    c_low = ((c[rank:] + nt(m_low, xh)) * root).astype(BF16)
    r = nt(hm_high, xh) + nt(hm_high, xl) + nt(hm_low, xh)
    r_up = jnp.where(sub < old, r[:rank], 0.0).astype(BF16)
    w_high, w_low = halves(r[rank:])
    r_low = (-(nn(kt[...], w_high) + nn(kt[...], w_low))).astype(BF16)
    for copy in [*loads[4:], *ui_loads]:
        copy.wait()
    step = rows // q_sem.shape[0]
    stores = []
    for t in range(rows // step):
        at = pl.ds(t * step, step)
        u, v = u_ref[at, :], v_ref[at, :]
        ui, uj = uit_ref[:, at], ujt[:, at]
        q_ref[at, :] = (nn(u, c_up) + tn(ui, c_low)).astype(BF16)
        stores.append(pltpu.make_async_copy(q_ref.at[at], q_hbm.at[at], q_sem.at[t]))
        stores[-1].start()
        w_ref[at, :] = (nn(v, r_up) + tn(uj, r_low)).astype(BF16)
        stores.append(pltpu.make_async_copy(w_ref.at[at], w_hbm.at[at], w_sem.at[t]))
        stores[-1].start()
    for copy in stores:
        copy.wait()


def body(tile_basis, tile_coeffs, panel_basis, panel_coeffs, tile_rank, target_rank, panel_rank, owner_row):
    n_row, n_col = lax.axis_size("row"), lax.axis_size("col")
    u, v = tile_basis[0, 0], tile_coeffs[0, 0]
    pu, pv = panel_basis[0], panel_coeffs[0]
    rows, rank = u.shape

    lefts, rights = {0: pu}, {0: pv}

    def grow(have, bits):
        for bit in bits:
            for m in list(have):
                have[m | bit] = swap(have[m], "col", n_col, bit)
        return tuple(have.values())

    high = [n_col >> t for t in range(1, n_col.bit_length() - 1)]

    gates = {
        0: lambda s: grow(lefts, high) if s == 2 else (),
        1: lambda _: grow(rights, high),
        n_row // 2: lambda _: grow(lefts, [1]) + grow(rights, [1]),
    }
    us, vs = ring_gathers(pu, pv, "row", n_row, gates)
    ui_parts = [lefts[m] for m in range(n_col)]

    ujs = picked_left(us, owner_row, n_row, n_col)
    ujs = [ujs[0]] + [swap(ujs[m], "col", n_col, m) for m in range(1, n_col)]
    kts = coupled(vs, [rights[m] for m in range(n_col)], owner_row, n_row, n_col)
    h_high, h_low, core_up = gram_products(u, v, [after(ui_parts[0], kts[0]), *ui_parts[1:]])
    kts = [kts[0]] + [swap(kts[m], "col", n_col, m) for m in range(1, n_col)]

    out = jax.ShapeDtypeStruct((rows, rank), BF16)
    square = pltpu.VMEM((rank, rank), F32)
    tall, wide = pltpu.VMEM((rows, rank), BF16), pltpu.VMEM((rank, rows), BF16)
    tiles = rows // 256 if rows % 256 == 0 else 1
    fresh_basis, fresh_coeffs = pl.pallas_call(
        functools.partial(finish, n_col),
        out_shape=(out, out),
        in_specs=[SMEM] * 4 + [HBM] * (5 + 2 * n_col) + [VMEM] * n_col,
        out_specs=(HBM, HBM),
        scratch_shapes=[
            tall,
            tall,
            wide,
            pltpu.VMEM((2 * rank, 2 * rank), BF16),
            pltpu.VMEM((2 * rank, 2 * rank), BF16),
            square,
            wide,
            tall,
            tall,
            pltpu.VMEM((rank, rank), BF16),
            pltpu.VMEM((2 * rank, rank), BF16),
            square,
            square,
            square,
            pltpu.SemaphoreType.DMA((5,)),
            pltpu.SemaphoreType.DMA((n_col,)),
            pltpu.SemaphoreType.DMA((n_col,)),
            pltpu.SemaphoreType.DMA((tiles,)),
            pltpu.SemaphoreType.DMA((tiles,)),
        ],
        compiler_params=pltpu.CompilerParams(vmem_limit_bytes=40 << 20),
        cost_estimate=pl.CostEstimate(flops=8 << 30, bytes_accessed=12 << 20, transcendentals=0),
        name="finish",
    )(tile_rank, target_rank, panel_rank, owner_row, u, v, h_high, h_low, core_up, *ui_parts, *ujs, *kts)
    return fresh_basis[None, None], fresh_coeffs[None, None]


def solution(mesh):
    tiles, panels = P("row", "col", None, None), P("row", "col", None)
    return jax.shard_map(
        body,
        mesh=mesh,
        in_specs=(tiles, tiles, panels, panels, P("row", "col"), P("row", "col"), P(), P()),
        out_specs=(tiles, tiles),
        check_vma=False,
    )
```

```python
import functools
import math

import jax
import jax.numpy as jnp
from jax import lax
from jax.experimental import pallas as pl
from jax.experimental.pallas import tpu as pltpu
from jax.sharding import PartitionSpec as P

F32 = jnp.float32
BF16 = jnp.bfloat16
VMEM = pl.BlockSpec(memory_space=pltpu.VMEM)
SMEM = pl.BlockSpec(memory_space=pltpu.SMEM)
HBM = pl.BlockSpec(memory_space=pltpu.HBM)
ROUGH, FINE = 0.05, 0.015
ROUGH_STEPS, FINE_STEPS = 12, 6


def nn(a, b):
    return lax.dot_general(a, b, (((1,), (0,)), ((), ())), preferred_element_type=F32)


def nt(a, b):
    return lax.dot_general(a, b, (((1,), (1,)), ((), ())), preferred_element_type=F32)


def tn(a, b):
    return lax.dot_general(a, b, (((0,), (0,)), ((), ())), preferred_element_type=F32)


def halves(x):
    high = x.astype(BF16)
    return high, (x - high.astype(F32)).astype(BF16)


def after(x, *others):
    return lax.optimization_barrier((x, *others))[0]


def ring_place(r, n):
    return jnp.where(r % 2 == 0, r // 2, n - 1 - r // 2)


def ring_steps(n):
    ring = list(range(0, n, 2)) + list(range(n - 1, 0, -2))
    ahead = [(ring[i], ring[(i + 1) % n]) for i in range(n)]
    return ahead, [(b, a) for a, b in ahead]


def ring_gathers(left, right, axis, n, gates):
    ahead, back = ring_steps(n)
    half, low = n // 2, left.shape[0] // 2
    lists = [[panel] + [None] * (n - 1) for panel in (left, right)]
    now = [(left, left), (right, right)]

    def step(panel, s, *gate):
        fwd, bwd, *_ = lax.optimization_barrier((*now[panel], *gate))
        if s == half:
            fwd, bwd = fwd[:low], bwd[low:]
        fwd, bwd = lax.ppermute(fwd, axis, ahead), lax.ppermute(bwd, axis, back)
        now[panel] = fwd, bwd
        if s == half:
            lists[panel][half] = fwd
            lists[panel].append(bwd)
        else:
            lists[panel][s], lists[panel][n - s] = fwd, bwd
        return fwd, bwd

    for s in range(1, half - 1):
        done = step(0, s, *(gates[0](s) if s > 1 else ()))
    for s in range(1, half + 1):
        if s < 3:
            early = step(0, half - 2 + s)
        gate = gates[s](lists) if s in gates else ()
        step(1, s, *gate, *(done if s < 3 else ()))
        done = early
    return lists


def swap(x, axis, n, m):
    return lax.ppermute(x, axis, [(i, i ^ m) for i in range(n)])


def assemble(parts, target):
    shard = target.shape[0] // len(parts)
    col = lax.axis_index("col")
    for m, part in enumerate(parts):
        target[pl.ds(pl.multiple_of((col ^ m) * shard, shard), shard), :] = part[...]


def owner_steps(n_row, n_col, owner):
    row, col = lax.axis_index("row"), lax.axis_index("col")
    here = ring_place(row, n_row)
    return [lax.rem(here - ring_place(owner[col ^ m], n_row) + n_row, n_row) for m in range(n_col)]


def pick(pieces, n_row, n_col, owner, outs):
    low = pieces[0].shape[0] // 2
    for m, step in enumerate(owner_steps(n_row, n_col, owner)):
        for k in range(n_row):

            @pl.when(step == k)
            def _():
                if k == n_row // 2:
                    outs[m][:low] = pieces[k][...]
                    outs[m][low:] = pieces[n_row][...]
                else:
                    outs[m][...] = pieces[k][...]


def pick_left(n_row, n_col, owner, *refs):
    pick(refs[: n_row + 1], n_row, n_col, owner, refs[n_row + 1 :])


def picked_left(pieces, owner, n_row, n_col):
    shard, width = pieces[0].shape
    return pl.pallas_call(
        functools.partial(pick_left, n_row, n_col),
        out_shape=[jax.ShapeDtypeStruct((shard, width), BF16)] * n_col,
        in_specs=[SMEM] + [VMEM] * (n_row + 1),
        out_specs=[VMEM] * n_col,
        compiler_params=pltpu.CompilerParams(vmem_limit_bytes=8 << 20),
        cost_estimate=pl.CostEstimate(flops=0, bytes_accessed=3 << 20, transcendentals=0),
        name="pick_left",
    )(owner, *pieces)


def couple(n_row, n_col, owner, *refs):
    pieces, parts = refs[: n_row + 1], refs[n_row + 1 : n_row + 1 + n_col]
    outs = refs[n_row + 1 + n_col : n_row + 1 + 2 * n_col]
    picked, mine = refs[n_row + 1 + 2 * n_col :]
    shard = pieces[0].shape[0]
    col = lax.axis_index("col")
    for m in range(n_col):
        mine[pl.ds(pl.multiple_of((col ^ m) * shard, shard), shard), :] = parts[m][...]
    pick(pieces, n_row, n_col, owner, [picked.at[pl.ds(m * shard, shard)] for m in range(n_col)])
    product = nt(picked[...], mine[...]).astype(BF16)
    for m in range(n_col):
        outs[m][...] = product[m * shard : (m + 1) * shard]


def coupled(pieces, parts, owner, n_row, n_col):
    shard, width = pieces[0].shape
    rank = n_col * shard
    return pl.pallas_call(
        functools.partial(couple, n_row, n_col),
        out_shape=[jax.ShapeDtypeStruct((shard, rank), BF16)] * n_col,
        in_specs=[SMEM] + [VMEM] * (n_row + 1 + n_col),
        out_specs=[VMEM] * n_col,
        scratch_shapes=[pltpu.VMEM((rank, width), BF16), pltpu.VMEM((rank, width), BF16)],
        compiler_params=pltpu.CompilerParams(vmem_limit_bytes=12 << 20),
        cost_estimate=pl.CostEstimate(flops=2 * rank * rank * width, bytes_accessed=3 << 20, transcendentals=0),
        name="coupling",
    )(owner, *pieces, *parts)


def grams(n_col, u_ref, v_ref, *refs):
    high, low, cu_ref, uit = refs[n_col:]
    rank = cu_ref.shape[0]
    assemble(refs[:n_col], uit)
    top, bottom = pl.ds(0, rank), pl.ds(rank, rank)

    def put(at, lanes, value):
        high[at, lanes], low[at, lanes] = halves(value)

    cu_ref[...] = tn(v_ref[...], v_ref[...])
    put(top, top, tn(u_ref[...], u_ref[...]))
    cross = nn(uit[...], u_ref[...])
    put(bottom, top, cross)
    put(top, bottom, cross.T)
    put(bottom, bottom, nt(uit[...], uit[...]))


def gram_products(u, v, parts):
    rows, rank = u.shape
    return pl.pallas_call(
        functools.partial(grams, len(parts)),
        out_shape=[jax.ShapeDtypeStruct((2 * rank, 2 * rank), BF16)] * 2 + [jax.ShapeDtypeStruct((rank, rank), F32)],
        in_specs=[VMEM] * (2 + len(parts)),
        out_specs=[VMEM] * 3,
        scratch_shapes=[pltpu.VMEM((rank, rows), BF16)],
        compiler_params=pltpu.CompilerParams(vmem_limit_bytes=24 << 20),
        cost_estimate=pl.CostEstimate(flops=8 * rank * rank * rows, bytes_accessed=6 << 20, transcendentals=0),
        name="grams",
    )(u, v, *parts)


def lower_half(e, eye, below):
    return jnp.where(below, e, jnp.where(eye, 0.5 * e, 0.0))


def finish(n_col, old_ref, goal_ref, panel, owner, u_ref, v_ref, hh, hl, cu_ref, *refs):
    ui_in, ujt_in, kt_in = refs[:n_col], refs[n_col : 2 * n_col], refs[2 * n_col : 3 * n_col]
    q_hbm, w_hbm, uit_ref, ujt, q_ref, w_ref, kt, mh, gn, y_ref, a_ref, q_sem, w_sem = refs[3 * n_col :]
    rows, rank = u_ref.shape
    row, col = lax.axis_index("row"), lax.axis_index("col")
    old, goal, here, there = old_ref[0, 0], goal_ref[0, 0], panel[row], panel[owner[col]]
    sub = lax.broadcasted_iota(jnp.int32, (rank, rank), 0)
    lane = lax.broadcasted_iota(jnp.int32, (rank, rank), 1)
    eye, below = sub == lane, sub > lane
    one = jnp.where(eye, 1.0, 0.0).astype(F32)
    assemble(kt_in, kt)
    assemble(ujt_in, ujt)
    zero = jnp.zeros((rank, rank), F32)
    kt[...] = jnp.where((sub < there) & (lane < here), kt[...].astype(F32), zero).astype(BF16)
    cl = jnp.where(lane < goal, nn(ujt[...], v_ref[...]), zero).astype(BF16)
    cu = jnp.where((sub < old) & (lane < goal), cu_ref[...], zero).astype(BF16)
    m_high, m_low = halves(-tn(kt[...], cl))
    mh[pl.ds(0, rank), :], mh[pl.ds(rank, rank), :] = cu, m_high
    hm = nn(hh[...], mh[...]) + nn(hl[...], mh[...]) + nn(hh[:, rank:], m_low)
    hm_high, hm_low = halves(hm)
    g = tn(mh[...], hm_high) + tn(mh[...], hm_low) + tn(m_low, hm_high[rank:])
    g = g + jnp.where(eye & (lane >= goal), 1.0, 0.0)
    dg = jnp.where(eye, g, 0.0)
    d_row = lax.rsqrt(jnp.sum(dg, axis=0, keepdims=True))
    d_col = lax.rsqrt(jnp.sum(dg, axis=1, keepdims=True))
    g = g * d_col * d_row
    gn[...] = g
    scale = rank / jnp.sum(g * g, keepdims=True)
    a_ref[...] = g * scale
    y_ref[...] = one * jnp.sqrt(scale)

    def rough(carry):
        step, _ = carry
        a = a_ref[...]
        e = a - one
        f = lower_half(e, eye, below).astype(BF16)
        y = y_ref[...]
        t = a - nn(f, a.astype(BF16))
        y_ref[...] = y - nn(f, y.astype(BF16))
        a_ref[...] = t - nt(t.astype(BF16), f)
        return step + 1, jnp.max(jnp.abs(e))

    def fine(carry):
        step, _ = carry
        y = y_ref[...]
        yh, yl = halves(y)
        gh, gl = halves(gn[...])
        th, tl = halves(nn(yh, gh) + nn(yh, gl) + nn(yl, gh))
        e = nt(th, yh) + nt(th, yl) + nt(tl, yh) - one
        y_ref[...] = y - nn(lower_half(e, eye, below).astype(BF16), yh)
        return step + 1, jnp.max(jnp.abs(e))

    lax.while_loop(lambda c: (c[0] < ROUGH_STEPS) & (c[1] > ROUGH), rough, (jnp.int32(0), F32(1.0)))
    _, err = lax.while_loop(lambda c: (c[0] < FINE_STEPS) & (c[1] > FINE), fine, (jnp.int32(0), F32(1.0)))
    lowest = jnp.min(jnp.where(eye, y_ref[...], 1.0))

    @pl.when(jnp.logical_not((err <= FINE) & (lowest > 0.0)))
    def _():
        a_ref[...] = gn[...]
        y_ref[...] = one

        def pivot(k, _):
            col = jnp.sum(jnp.where(lane == k, a_ref[...], 0.0), axis=1, keepdims=True)
            row = jnp.sum(jnp.where(sub == k, a_ref[...], 0.0), axis=0, keepdims=True)
            yrow = jnp.sum(jnp.where(sub == k, y_ref[...], 0.0), axis=0, keepdims=True)
            top = jnp.sum(jnp.where(lax.broadcasted_iota(jnp.int32, (1, rank), 1) == k, row, 0.0))
            inv = 1.0 / jnp.sqrt(jnp.full((1, rank), top))
            row, yrow = row * inv, yrow * inv
            col = jnp.where(lax.broadcasted_iota(jnp.int32, (rank, 1), 0) > k, col * inv[:, :1], 0.0)
            a_ref[...] = a_ref[...] - col * row
            y_ref[...] = jnp.where(sub == k, yrow, y_ref[...] - col * yrow)
            return 0

        lax.fori_loop(0, rank, pivot, 0)

    xh, xl = halves(y_ref[...] * d_row)
    root = math.sqrt(rows)
    c = nt(mh[...], xh) + nt(mh[...], xl)
    c_up = (c[:rank] * root).astype(BF16)
    c_low = ((c[rank:] + nt(m_low, xh)) * root).astype(BF16)
    r = nt(hm_high, xh) + nt(hm_high, xl) + nt(hm_low, xh)
    r_up = jnp.where(sub < old, r[:rank], 0.0).astype(BF16)
    w_high, w_low = halves(r[rank:])
    r_low = (-(nn(kt[...], w_high) + nn(kt[...], w_low))).astype(BF16)
    assemble(ui_in, uit_ref)
    step = rows // q_sem.shape[0]
    stores = []
    for t in range(rows // step):
        at = pl.ds(t * step, step)
        u, v = u_ref[at, :], v_ref[at, :]
        ui, uj = uit_ref[:, at], ujt[:, at]
        q_ref[at, :] = (nn(u, c_up) + tn(ui, c_low)).astype(BF16)
        stores.append(pltpu.make_async_copy(q_ref.at[at], q_hbm.at[at], q_sem.at[t]))
        stores[-1].start()
        w_ref[at, :] = (nn(v, r_up) + tn(uj, r_low)).astype(BF16)
        stores.append(pltpu.make_async_copy(w_ref.at[at], w_hbm.at[at], w_sem.at[t]))
        stores[-1].start()
    for copy in stores:
        copy.wait()


def body(tile_basis, tile_coeffs, panel_basis, panel_coeffs, tile_rank, target_rank, panel_rank, owner_row):
    n_row, n_col = lax.axis_size("row"), lax.axis_size("col")
    u, v = tile_basis[0, 0], tile_coeffs[0, 0]
    pu, pv = panel_basis[0], panel_coeffs[0]
    rows, rank = u.shape

    lefts, rights = {0: pu}, {0: pv}

    def grow(have, bits):
        for bit in bits:
            for m in list(have):
                have[m | bit] = swap(have[m], "col", n_col, bit)
        return tuple(have.values())

    high = [n_col >> t for t in range(1, n_col.bit_length() - 1)]

    gates = {
        0: lambda s: grow(lefts, high) if s == 2 else (),
        1: lambda _: grow(rights, high),
        n_row // 2: lambda _: grow(lefts, [1]) + grow(rights, [1]),
    }
    us, vs = ring_gathers(pu, pv, "row", n_row, gates)
    ui_parts = [lefts[m] for m in range(n_col)]

    ujs = picked_left(us, owner_row, n_row, n_col)
    ujs = [ujs[0]] + [swap(ujs[m], "col", n_col, m) for m in range(1, n_col)]
    kts = coupled(vs, [rights[m] for m in range(n_col)], owner_row, n_row, n_col)
    h_high, h_low, core_up = gram_products(u, v, [after(ui_parts[0], kts[0]), *ui_parts[1:]])
    kts = [kts[0]] + [swap(kts[m], "col", n_col, m) for m in range(1, n_col)]

    out = jax.ShapeDtypeStruct((rows, rank), BF16)
    square = pltpu.VMEM((rank, rank), F32)
    tall, wide = pltpu.VMEM((rows, rank), BF16), pltpu.VMEM((rank, rows), BF16)
    tiles = rows // 256 if rows % 256 == 0 else 1
    fresh_basis, fresh_coeffs = pl.pallas_call(
        functools.partial(finish, n_col),
        out_shape=(out, out),
        in_specs=[SMEM] * 4 + [VMEM] * (5 + 3 * n_col),
        out_specs=(HBM, HBM),
        scratch_shapes=[
            wide,
            wide,
            tall,
            tall,
            pltpu.VMEM((rank, rank), BF16),
            pltpu.VMEM((2 * rank, rank), BF16),
            square,
            square,
            square,
            pltpu.SemaphoreType.DMA((tiles,)),
            pltpu.SemaphoreType.DMA((tiles,)),
        ],
        compiler_params=pltpu.CompilerParams(vmem_limit_bytes=24 << 20),
        cost_estimate=pl.CostEstimate(flops=8 << 30, bytes_accessed=12 << 20, transcendentals=0),
        name="finish",
    )(tile_rank, target_rank, panel_rank, owner_row, u, v, h_high, h_low, core_up, *ui_parts, *ujs, *kts)
    return fresh_basis[None, None], fresh_coeffs[None, None]


def solution(mesh):
    tiles, panels = P("row", "col", None, None), P("row", "col", None)
    return jax.shard_map(
        body,
        mesh=mesh,
        in_specs=(tiles, tiles, panels, panels, P("row", "col"), P("row", "col"), P(), P()),
        out_specs=(tiles, tiles),
        check_vma=False,
    )
```

```python
import functools
import math

import jax
import jax.numpy as jnp
from jax import lax
from jax.experimental import pallas as pl
from jax.experimental.pallas import tpu as pltpu
from jax.sharding import PartitionSpec as P

F32 = jnp.float32
BF16 = jnp.bfloat16
VMEM = pl.BlockSpec(memory_space=pltpu.VMEM)
SMEM = pl.BlockSpec(memory_space=pltpu.SMEM)
HBM = pl.BlockSpec(memory_space=pltpu.HBM)
ROUGH, FINE = 0.05, 0.015
ROUGH_STEPS, FINE_STEPS = 12, 6


def nn(a, b):
    return lax.dot_general(a, b, (((1,), (0,)), ((), ())), preferred_element_type=F32)


def nt(a, b):
    return lax.dot_general(a, b, (((1,), (1,)), ((), ())), preferred_element_type=F32)


def tn(a, b):
    return lax.dot_general(a, b, (((0,), (0,)), ((), ())), preferred_element_type=F32)


def halves(x):
    high = x.astype(BF16)
    return high, (x - high.astype(F32)).astype(BF16)


def after(x, *others):
    return lax.optimization_barrier((x, *others))[0]


def ring_place(r, n):
    return jnp.where(r % 2 == 0, r // 2, n - 1 - r // 2)


def ring_steps(n):
    ring = list(range(0, n, 2)) + list(range(n - 1, 0, -2))
    ahead = [(ring[i], ring[(i + 1) % n]) for i in range(n)]
    return ahead, [(b, a) for a, b in ahead]


def ring_gathers(left, right, axis, n, gates):
    ahead, back = ring_steps(n)
    half, low = n // 2, left.shape[0] // 2
    lists = [[panel] + [None] * (n - 1) for panel in (left, right)]
    now = [(left, left), (right, right)]

    def step(panel, s, *gate):
        fwd, bwd, *_ = lax.optimization_barrier((*now[panel], *gate))
        if s == half:
            fwd, bwd = fwd[:low], bwd[low:]
        fwd, bwd = lax.ppermute(fwd, axis, ahead), lax.ppermute(bwd, axis, back)
        now[panel] = fwd, bwd
        if s == half:
            lists[panel][half] = fwd
            lists[panel].append(bwd)
        else:
            lists[panel][s], lists[panel][n - s] = fwd, bwd
        return fwd, bwd

    for s in range(1, half - 1):
        done = step(0, s, *(gates[0](s) if s > 1 else ()))
    for s in range(1, half + 1):
        if s < 3:
            early = step(0, half - 2 + s)
        gate = gates[s](lists) if s in gates else ()
        step(1, s, *gate, *(done if s < 2 else ()))
        done = early
    return lists


def swap(x, axis, n, m):
    return lax.ppermute(x, axis, [(i, i ^ m) for i in range(n)])


def assemble(parts, target):
    shard = target.shape[0] // len(parts)
    col = lax.axis_index("col")
    for m, part in enumerate(parts):
        target[pl.ds(pl.multiple_of((col ^ m) * shard, shard), shard), :] = part[...]


def owner_steps(n_row, n_col, owner):
    row, col = lax.axis_index("row"), lax.axis_index("col")
    here = ring_place(row, n_row)
    return [lax.rem(here - ring_place(owner[col ^ m], n_row) + n_row, n_row) for m in range(n_col)]


def pick(pieces, n_row, n_col, owner, outs):
    low = pieces[0].shape[0] // 2
    for m, step in enumerate(owner_steps(n_row, n_col, owner)):
        for k in range(n_row):

            @pl.when(step == k)
            def _():
                if k == n_row // 2:
                    outs[m][:low] = pieces[k][...]
                    outs[m][low:] = pieces[n_row][...]
                else:
                    outs[m][...] = pieces[k][...]


def pick_left(n_row, n_col, owner, *refs):
    pick(refs[: n_row + 1], n_row, n_col, owner, refs[n_row + 1 :])


def picked_left(pieces, owner, n_row, n_col):
    shard, width = pieces[0].shape
    return pl.pallas_call(
        functools.partial(pick_left, n_row, n_col),
        out_shape=[jax.ShapeDtypeStruct((shard, width), BF16)] * n_col,
        in_specs=[SMEM] + [VMEM] * (n_row + 1),
        out_specs=[VMEM] * n_col,
        compiler_params=pltpu.CompilerParams(vmem_limit_bytes=8 << 20),
        cost_estimate=pl.CostEstimate(flops=0, bytes_accessed=3 << 20, transcendentals=0),
        name="pick_left",
    )(owner, *pieces)


def couple(n_row, n_col, owner, *refs):
    pieces, parts = refs[: n_row + 1], refs[n_row + 1 : n_row + 1 + n_col]
    outs = refs[n_row + 1 + n_col : n_row + 1 + 2 * n_col]
    picked, mine = refs[n_row + 1 + 2 * n_col :]
    shard = pieces[0].shape[0]
    col = lax.axis_index("col")
    for m in range(n_col):
        mine[pl.ds(pl.multiple_of((col ^ m) * shard, shard), shard), :] = parts[m][...]
    pick(pieces, n_row, n_col, owner, [picked.at[pl.ds(m * shard, shard)] for m in range(n_col)])
    product = nt(picked[...], mine[...]).astype(BF16)
    for m in range(n_col):
        outs[m][...] = product[m * shard : (m + 1) * shard]


def coupled(pieces, parts, owner, n_row, n_col):
    shard, width = pieces[0].shape
    rank = n_col * shard
    return pl.pallas_call(
        functools.partial(couple, n_row, n_col),
        out_shape=[jax.ShapeDtypeStruct((shard, rank), BF16)] * n_col,
        in_specs=[SMEM] + [VMEM] * (n_row + 1 + n_col),
        out_specs=[VMEM] * n_col,
        scratch_shapes=[pltpu.VMEM((rank, width), BF16), pltpu.VMEM((rank, width), BF16)],
        compiler_params=pltpu.CompilerParams(vmem_limit_bytes=12 << 20),
        cost_estimate=pl.CostEstimate(flops=2 * rank * rank * width, bytes_accessed=3 << 20, transcendentals=0),
        name="coupling",
    )(owner, *pieces, *parts)


def grams(n_col, old_ref, goal_ref, u_ref, v_ref, *refs):
    high, low, cu_ref, hm_ref, g_ref, uit = refs[n_col:]
    rank = cu_ref.shape[0]
    sub = lax.broadcasted_iota(jnp.int32, (rank, rank), 0)
    lane = lax.broadcasted_iota(jnp.int32, (rank, rank), 1)
    assemble(refs[:n_col], uit)
    top, bottom = pl.ds(0, rank), pl.ds(rank, rank)
    kept = (sub < old_ref[0, 0]) & (lane < goal_ref[0, 0])
    cu = jnp.where(kept, tn(v_ref[...], v_ref[...]), 0.0).astype(BF16)
    cu_ref[...] = cu
    first_high, first_low = halves(tn(u_ref[...], u_ref[...]))
    hm = nn(first_high, cu) + nn(first_low, cu)
    hm_ref[top, :] = hm
    hm_high, hm_low = halves(hm)
    g_ref[...] = tn(cu, hm_high) + tn(cu, hm_low)
    cross = nn(uit[...], u_ref[...])
    cross_high, cross_low = halves(cross)
    hm_ref[bottom, :] = nn(cross_high, cu) + nn(cross_low, cu)
    high[top, :], low[top, :] = halves(cross.T)
    high[bottom, :], low[bottom, :] = halves(nt(uit[...], uit[...]))


def gram_products(old, goal, u, v, parts):
    rows, rank = u.shape
    return pl.pallas_call(
        functools.partial(grams, len(parts)),
        out_shape=[
            jax.ShapeDtypeStruct((2 * rank, rank), BF16),
            jax.ShapeDtypeStruct((2 * rank, rank), BF16),
            jax.ShapeDtypeStruct((rank, rank), BF16),
            jax.ShapeDtypeStruct((2 * rank, rank), F32),
            jax.ShapeDtypeStruct((rank, rank), F32),
            jax.ShapeDtypeStruct((rank, rows), BF16),
        ],
        in_specs=[SMEM] * 2 + [VMEM] * (2 + len(parts)),
        out_specs=[VMEM] * 6,
        compiler_params=pltpu.CompilerParams(vmem_limit_bytes=24 << 20),
        cost_estimate=pl.CostEstimate(flops=8 * rank * rank * rows, bytes_accessed=6 << 20, transcendentals=0),
        name="grams",
    )(old, goal, u, v, *parts)


def lower_half(e, eye, below):
    return jnp.where(below, e, jnp.where(eye, 0.5 * e, 0.0))


def finish(n_col, old_ref, goal_ref, panel, owner, u_ref, v_ref, hh, hl, cu_ref, hm_ref, g_ref, uit_ref, *refs):
    ujt_in, kt_in = refs[:n_col], refs[n_col : 2 * n_col]
    q_hbm, w_hbm, ujt, q_ref, w_ref, kt, mh, gn, y_ref, a_ref, q_sem, w_sem = refs[2 * n_col :]
    rows, rank = u_ref.shape
    row, col = lax.axis_index("row"), lax.axis_index("col")
    old, goal, here, there = old_ref[0, 0], goal_ref[0, 0], panel[row], panel[owner[col]]
    sub = lax.broadcasted_iota(jnp.int32, (rank, rank), 0)
    lane = lax.broadcasted_iota(jnp.int32, (rank, rank), 1)
    eye, below = sub == lane, sub > lane
    one = jnp.where(eye, 1.0, 0.0).astype(F32)
    assemble(kt_in, kt)
    assemble(ujt_in, ujt)
    zero = jnp.zeros((rank, rank), F32)
    kt[...] = jnp.where((sub < there) & (lane < here), kt[...].astype(F32), zero).astype(BF16)
    cl = jnp.where(lane < goal, nn(ujt[...], v_ref[...]), zero).astype(BF16)
    cu = cu_ref[...]
    m_high, m_low = halves(-tn(kt[...], cl))
    mh[pl.ds(0, rank), :], mh[pl.ds(rank, rank), :] = cu, m_high
    more = nn(hh[...], m_high) + nn(hh[...], m_low) + nn(hl[...], m_high)
    more_high, more_low = halves(more)
    mixed = tn(cu, more_high[:rank]) + tn(cu, more_low[:rank])
    own = tn(m_high, more_high[rank:]) + tn(m_high, more_low[rank:]) + tn(m_low, more_high[rank:])
    g = g_ref[...] + mixed + mixed.T + own
    hm_high, hm_low = halves(hm_ref[...] + more)
    g = g + jnp.where(eye & (lane >= goal), 1.0, 0.0)
    dg = jnp.where(eye, g, 0.0)
    d_row = lax.rsqrt(jnp.sum(dg, axis=0, keepdims=True))
    d_col = lax.rsqrt(jnp.sum(dg, axis=1, keepdims=True))
    g = g * d_col * d_row
    gn[...] = g
    scale = rank / jnp.sum(g * g, keepdims=True)
    a_ref[...] = g * scale
    y_ref[...] = one * jnp.sqrt(scale)

    def rough(carry):
        step, _ = carry
        a = a_ref[...]
        e = a - one
        f = lower_half(e, eye, below).astype(BF16)
        y = y_ref[...]
        t = a - nn(f, a.astype(BF16))
        y_ref[...] = y - nn(f, y.astype(BF16))
        a_ref[...] = t - nt(t.astype(BF16), f)
        return step + 1, jnp.max(jnp.abs(e))

    def fine(carry):
        step, _ = carry
        y = y_ref[...]
        yh, yl = halves(y)
        gh, gl = halves(gn[...])
        th, tl = halves(nn(yh, gh) + nn(yh, gl) + nn(yl, gh))
        e = nt(th, yh) + nt(th, yl) + nt(tl, yh) - one
        y_ref[...] = y - nn(lower_half(e, eye, below).astype(BF16), yh)
        return step + 1, jnp.max(jnp.abs(e))

    lax.while_loop(lambda c: (c[0] < ROUGH_STEPS) & (c[1] > ROUGH), rough, (jnp.int32(0), F32(1.0)))
    _, err = lax.while_loop(lambda c: (c[0] < FINE_STEPS) & (c[1] > FINE), fine, (jnp.int32(0), F32(1.0)))
    lowest = jnp.min(jnp.where(eye, y_ref[...], 1.0))

    @pl.when(jnp.logical_not((err <= FINE) & (lowest > 0.0)))
    def _():
        a_ref[...] = gn[...]
        y_ref[...] = one

        def pivot(k, _):
            col = jnp.sum(jnp.where(lane == k, a_ref[...], 0.0), axis=1, keepdims=True)
            row = jnp.sum(jnp.where(sub == k, a_ref[...], 0.0), axis=0, keepdims=True)
            yrow = jnp.sum(jnp.where(sub == k, y_ref[...], 0.0), axis=0, keepdims=True)
            top = jnp.sum(jnp.where(lax.broadcasted_iota(jnp.int32, (1, rank), 1) == k, row, 0.0))
            inv = 1.0 / jnp.sqrt(jnp.full((1, rank), top))
            row, yrow = row * inv, yrow * inv
            col = jnp.where(lax.broadcasted_iota(jnp.int32, (rank, 1), 0) > k, col * inv[:, :1], 0.0)
            a_ref[...] = a_ref[...] - col * row
            y_ref[...] = jnp.where(sub == k, yrow, y_ref[...] - col * yrow)
            return 0

        lax.fori_loop(0, rank, pivot, 0)

    xh, xl = halves(y_ref[...] * d_row)
    root = math.sqrt(rows)
    c = nt(mh[...], xh) + nt(mh[...], xl)
    c_up = (c[:rank] * root).astype(BF16)
    c_low = ((c[rank:] + nt(m_low, xh)) * root).astype(BF16)
    r = nt(hm_high, xh) + nt(hm_high, xl) + nt(hm_low, xh)
    r_up = jnp.where(sub < old, r[:rank], 0.0).astype(BF16)
    w_high, w_low = halves(r[rank:])
    r_low = (-(nn(kt[...], w_high) + nn(kt[...], w_low))).astype(BF16)
    step = rows // q_sem.shape[0]
    stores = []
    for t in range(rows // step):
        at = pl.ds(t * step, step)
        u, v = u_ref[at, :], v_ref[at, :]
        ui, uj = uit_ref[:, at], ujt[:, at]
        q_ref[at, :] = (nn(u, c_up) + tn(ui, c_low)).astype(BF16)
        stores.append(pltpu.make_async_copy(q_ref.at[at], q_hbm.at[at], q_sem.at[t]))
        stores[-1].start()
        w_ref[at, :] = (nn(v, r_up) + tn(uj, r_low)).astype(BF16)
        stores.append(pltpu.make_async_copy(w_ref.at[at], w_hbm.at[at], w_sem.at[t]))
        stores[-1].start()
    for copy in stores:
        copy.wait()


def body(tile_basis, tile_coeffs, panel_basis, panel_coeffs, tile_rank, target_rank, panel_rank, owner_row):
    n_row, n_col = lax.axis_size("row"), lax.axis_size("col")
    u, v = tile_basis[0, 0], tile_coeffs[0, 0]
    pu, pv = panel_basis[0], panel_coeffs[0]
    rows, rank = u.shape

    lefts, rights = {0: pu}, {0: pv}

    def grow(have, bits):
        for bit in bits:
            for m in list(have):
                have[m | bit] = swap(have[m], "col", n_col, bit)
        return tuple(have.values())

    high = [n_col >> t for t in range(1, n_col.bit_length() - 1)]

    gates = {
        0: lambda s: grow(lefts, high) if s == 2 else (),
        1: lambda _: grow(rights, high),
        n_row // 2: lambda _: grow(lefts, [1]) + grow(rights, [1]),
    }
    us, vs = ring_gathers(pu, pv, "row", n_row, gates)
    ui_parts = [lefts[m] for m in range(n_col)]

    ujs = picked_left(us, owner_row, n_row, n_col)
    ujs = [ujs[0]] + [swap(ujs[m], "col", n_col, m) for m in range(1, n_col)]
    kts = coupled(vs, [rights[m] for m in range(n_col)], owner_row, n_row, n_col)
    early = gram_products(tile_rank, target_rank, u, v, [after(ui_parts[0], kts[0]), *ui_parts[1:]])
    kts = [kts[0]] + [swap(kts[m], "col", n_col, m) for m in range(1, n_col)]

    out = jax.ShapeDtypeStruct((rows, rank), BF16)
    square = pltpu.VMEM((rank, rank), F32)
    tall, wide = pltpu.VMEM((rows, rank), BF16), pltpu.VMEM((rank, rows), BF16)
    tiles = rows // 256 if rows % 256 == 0 else 1
    fresh_basis, fresh_coeffs = pl.pallas_call(
        functools.partial(finish, n_col),
        out_shape=(out, out),
        in_specs=[SMEM] * 4 + [VMEM] * (8 + 2 * n_col),
        out_specs=(HBM, HBM),
        scratch_shapes=[
            wide,
            tall,
            tall,
            pltpu.VMEM((rank, rank), BF16),
            pltpu.VMEM((2 * rank, rank), BF16),
            square,
            square,
            square,
            pltpu.SemaphoreType.DMA((tiles,)),
            pltpu.SemaphoreType.DMA((tiles,)),
        ],
        compiler_params=pltpu.CompilerParams(vmem_limit_bytes=24 << 20),
        cost_estimate=pl.CostEstimate(flops=8 << 30, bytes_accessed=12 << 20, transcendentals=0),
        name="finish",
    )(tile_rank, target_rank, panel_rank, owner_row, u, v, *early, *ujs, *kts)
    return fresh_basis[None, None], fresh_coeffs[None, None]


def solution(mesh):
    tiles, panels = P("row", "col", None, None), P("row", "col", None)
    return jax.shard_map(
        body,
        mesh=mesh,
        in_specs=(tiles, tiles, panels, panels, P("row", "col"), P("row", "col"), P(), P()),
        out_specs=(tiles, tiles),
        check_vma=False,
    )
```

```python
import functools
import math

import jax
import jax.numpy as jnp
from jax import lax
from jax.experimental import pallas as pl
from jax.experimental.pallas import tpu as pltpu
from jax.sharding import PartitionSpec as P

F32 = jnp.float32
BF16 = jnp.bfloat16
VMEM = pl.BlockSpec(memory_space=pltpu.VMEM)
SMEM = pl.BlockSpec(memory_space=pltpu.SMEM)
HBM = pl.BlockSpec(memory_space=pltpu.HBM)
ROUGH, FINE = 0.05, 0.015
ROUGH_STEPS, FINE_STEPS = 12, 6


def nn(a, b):
    return lax.dot_general(a, b, (((1,), (0,)), ((), ())), preferred_element_type=F32)


def nt(a, b):
    return lax.dot_general(a, b, (((1,), (1,)), ((), ())), preferred_element_type=F32)


def tn(a, b):
    return lax.dot_general(a, b, (((0,), (0,)), ((), ())), preferred_element_type=F32)


def halves(x):
    high = x.astype(BF16)
    return high, (x - high.astype(F32)).astype(BF16)


def after(x, *others):
    return lax.optimization_barrier((x, *others))[0]


def ring_place(r, n):
    return jnp.where(r % 2 == 0, r // 2, n - 1 - r // 2)


def ring_steps(n):
    ring = list(range(0, n, 2)) + list(range(n - 1, 0, -2))
    ahead = [(ring[i], ring[(i + 1) % n]) for i in range(n)]
    return ahead, [(b, a) for a, b in ahead]


def ring_gathers(left, right, axis, n, gates):
    ahead, back = ring_steps(n)
    half, low = n // 2, left.shape[0] // 2
    lists = [[panel] + [None] * (n - 1) for panel in (left, right)]
    now = [(left, left), (right, right)]

    def step(panel, s, *gate):
        fwd, bwd, *_ = lax.optimization_barrier((*now[panel], *gate))
        if s == half:
            fwd, bwd = fwd[:low], bwd[low:]
        fwd, bwd = lax.ppermute(fwd, axis, ahead), lax.ppermute(bwd, axis, back)
        now[panel] = fwd, bwd
        if s == half:
            lists[panel][half] = fwd
            lists[panel].append(bwd)
        else:
            lists[panel][s], lists[panel][n - s] = fwd, bwd
        return fwd, bwd

    for s in range(1, half - 1):
        done = step(0, s, *(gates[0](s) if s > 1 else ()))
    for s in range(1, half + 1):
        if s < 3:
            early = step(0, half - 2 + s)
        gate = gates[s](lists) if s in gates else ()
        step(1, s, *gate, *(done if s < 2 else ()))
        done = early
    return lists


def swap(x, axis, n, m):
    return lax.ppermute(x, axis, [(i, i ^ m) for i in range(n)])


def assemble(parts, target):
    shard = target.shape[0] // len(parts)
    col = lax.axis_index("col")
    for m, part in enumerate(parts):
        target[pl.ds(pl.multiple_of((col ^ m) * shard, shard), shard), :] = part[...]


def owner_steps(n_row, n_col, owner):
    row, col = lax.axis_index("row"), lax.axis_index("col")
    here = ring_place(row, n_row)
    return [lax.rem(here - ring_place(owner[col ^ m], n_row) + n_row, n_row) for m in range(n_col)]


def pick(pieces, n_row, n_col, owner, outs):
    low = pieces[0].shape[0] // 2
    for m, step in enumerate(owner_steps(n_row, n_col, owner)):
        for k in range(n_row):

            @pl.when(step == k)
            def _():
                if k == n_row // 2:
                    outs[m][:low] = pieces[k][...]
                    outs[m][low:] = pieces[n_row][...]
                else:
                    outs[m][...] = pieces[k][...]


def pick_left(n_row, n_col, owner, *refs):
    pick(refs[: n_row + 1], n_row, n_col, owner, refs[n_row + 1 :])


def picked_left(pieces, owner, n_row, n_col):
    shard, width = pieces[0].shape
    return pl.pallas_call(
        functools.partial(pick_left, n_row, n_col),
        out_shape=[jax.ShapeDtypeStruct((shard, width), BF16)] * n_col,
        in_specs=[SMEM] + [VMEM] * (n_row + 1),
        out_specs=[VMEM] * n_col,
        compiler_params=pltpu.CompilerParams(vmem_limit_bytes=8 << 20),
        cost_estimate=pl.CostEstimate(flops=0, bytes_accessed=3 << 20, transcendentals=0),
        name="pick_left",
    )(owner, *pieces)


def couple(n_row, n_col, owner, *refs):
    pieces, parts = refs[: n_row + 1], refs[n_row + 1 : n_row + 1 + n_col]
    outs = refs[n_row + 1 + n_col : n_row + 1 + 2 * n_col]
    picked, mine = refs[n_row + 1 + 2 * n_col :]
    shard = pieces[0].shape[0]
    col = lax.axis_index("col")
    for m in range(n_col):
        mine[pl.ds(pl.multiple_of((col ^ m) * shard, shard), shard), :] = parts[m][...]
    pick(pieces, n_row, n_col, owner, [picked.at[pl.ds(m * shard, shard)] for m in range(n_col)])
    product = nt(picked[...], mine[...]).astype(BF16)
    for m in range(n_col):
        outs[m][...] = product[m * shard : (m + 1) * shard]


def coupled(pieces, parts, owner, n_row, n_col):
    shard, width = pieces[0].shape
    rank = n_col * shard
    return pl.pallas_call(
        functools.partial(couple, n_row, n_col),
        out_shape=[jax.ShapeDtypeStruct((shard, rank), BF16)] * n_col,
        in_specs=[SMEM] + [VMEM] * (n_row + 1 + n_col),
        out_specs=[VMEM] * n_col,
        scratch_shapes=[pltpu.VMEM((rank, width), BF16), pltpu.VMEM((rank, width), BF16)],
        compiler_params=pltpu.CompilerParams(vmem_limit_bytes=12 << 20),
        cost_estimate=pl.CostEstimate(flops=2 * rank * rank * width, bytes_accessed=3 << 20, transcendentals=0),
        name="coupling",
    )(owner, *pieces, *parts)


def grams(n_col, old_ref, goal_ref, u_ref, v_ref, *refs):
    high, low, cu_ref, hm_ref, g_ref, uit = refs[n_col:]
    rank = cu_ref.shape[0]
    sub = lax.broadcasted_iota(jnp.int32, (rank, rank), 0)
    lane = lax.broadcasted_iota(jnp.int32, (rank, rank), 1)
    assemble(refs[:n_col], uit)
    top, bottom = pl.ds(0, rank), pl.ds(rank, rank)
    kept = (sub < old_ref[0, 0]) & (lane < goal_ref[0, 0])
    cu = jnp.where(kept, tn(v_ref[...], v_ref[...]), 0.0).astype(BF16)
    cu_ref[...] = cu
    first_high, first_low = halves(tn(u_ref[...], u_ref[...]))
    hm = nn(first_high, cu) + nn(first_low, cu)
    hm_ref[top, :] = hm
    hm_high, hm_low = halves(hm)
    g_ref[...] = tn(cu, hm_high) + tn(cu, hm_low)
    cross = nn(uit[...], u_ref[...])
    cross_high, cross_low = halves(cross)
    hm_ref[bottom, :] = nn(cross_high, cu) + nn(cross_low, cu)
    high[top, :], low[top, :] = halves(cross.T)
    high[bottom, :], low[bottom, :] = halves(nt(uit[...], uit[...]))


def gram_products(old, goal, u, v, parts):
    rows, rank = u.shape
    return pl.pallas_call(
        functools.partial(grams, len(parts)),
        out_shape=[
            jax.ShapeDtypeStruct((2 * rank, rank), BF16),
            jax.ShapeDtypeStruct((2 * rank, rank), BF16),
            jax.ShapeDtypeStruct((rank, rank), BF16),
            jax.ShapeDtypeStruct((2 * rank, rank), F32),
            jax.ShapeDtypeStruct((rank, rank), F32),
            jax.ShapeDtypeStruct((rank, rows), BF16),
        ],
        in_specs=[SMEM] * 2 + [VMEM] * (2 + len(parts)),
        out_specs=[VMEM] * 6,
        compiler_params=pltpu.CompilerParams(vmem_limit_bytes=24 << 20),
        cost_estimate=pl.CostEstimate(flops=8 * rank * rank * rows, bytes_accessed=6 << 20, transcendentals=0),
        name="grams",
    )(old, goal, u, v, *parts)


def lower_half(e, eye, below):
    return jnp.where(below, e, jnp.where(eye, 0.5 * e, 0.0))


def finish(n_col, old_ref, goal_ref, panel, owner, u_ref, v_ref, hh, hl, cu_ref, hm_ref, g_ref, uit_ref, *refs):
    ujt_in, kt_in = refs[:n_col], refs[n_col : 2 * n_col]
    q_hbm, w_hbm, ujt, q_ref, w_ref, kt, mh, gn, y_ref, a_ref, q_sem, w_sem = refs[2 * n_col :]
    rows, rank = u_ref.shape
    row, col = lax.axis_index("row"), lax.axis_index("col")
    old, goal, here, there = old_ref[0, 0], goal_ref[0, 0], panel[row], panel[owner[col]]
    sub = lax.broadcasted_iota(jnp.int32, (rank, rank), 0)
    lane = lax.broadcasted_iota(jnp.int32, (rank, rank), 1)
    eye, below = sub == lane, sub > lane
    one = jnp.where(eye, 1.0, 0.0).astype(F32)
    assemble(kt_in, kt)
    assemble(ujt_in, ujt)
    zero = jnp.zeros((rank, rank), F32)
    kt[...] = jnp.where((sub < there) & (lane < here), kt[...].astype(F32), zero).astype(BF16)
    cl = jnp.where(lane < goal, nn(ujt[...], v_ref[...]), zero).astype(BF16)
    cu = cu_ref[...]
    m_high, m_low = halves(-tn(kt[...], cl))
    mh[pl.ds(0, rank), :], mh[pl.ds(rank, rank), :] = cu, m_high
    more = nn(hh[...], m_high) + nn(hh[...], m_low) + nn(hl[...], m_high)
    more_high, more_low = halves(more)
    mixed = tn(cu, more_high[:rank]) + tn(cu, more_low[:rank])
    own = tn(m_high, more_high[rank:]) + tn(m_high, more_low[rank:]) + tn(m_low, more_high[rank:])
    g = g_ref[...] + mixed + mixed.T + own
    hm_high, hm_low = halves(hm_ref[...] + more)
    g = g + jnp.where(eye & (lane >= goal), 1.0, 0.0)
    dg = jnp.where(eye, g, 0.0)
    d_row = lax.rsqrt(jnp.sum(dg, axis=0, keepdims=True))
    d_col = lax.rsqrt(jnp.sum(dg, axis=1, keepdims=True))
    g = g * d_col * d_row
    gn[...] = g
    scale = rank / jnp.sum(g * g, keepdims=True)
    a_ref[...] = g * scale
    y_ref[...] = one * jnp.sqrt(scale)

    def rough(carry):
        step, _ = carry
        a = a_ref[...]
        e = a - one
        f = lower_half(e, eye, below).astype(BF16)
        y = y_ref[...]
        t = a - nn(f, a.astype(BF16))
        y_ref[...] = y - nn(f, y.astype(BF16))
        a_ref[...] = t - nt(t.astype(BF16), f)
        return step + 1, jnp.max(jnp.abs(e))

    def fine(carry):
        step, _ = carry
        y = y_ref[...]
        yh, yl = halves(y)
        gh, gl = halves(gn[...])
        th, tl = halves(nn(yh, gh) + nn(yh, gl) + nn(yl, gh))
        e = nt(th, yh) + nt(th, yl) + nt(tl, yh) - one
        y_ref[...] = y - nn(lower_half(e, eye, below).astype(BF16), yh)
        return step + 1, jnp.max(jnp.abs(e))

    lax.while_loop(lambda c: (c[0] < ROUGH_STEPS) & (c[1] > ROUGH), rough, (jnp.int32(0), F32(1.0)))
    _, err = lax.while_loop(lambda c: (c[0] < FINE_STEPS) & (c[1] > FINE), fine, (jnp.int32(0), F32(1.0)))
    lowest = jnp.min(jnp.where(eye, y_ref[...], 1.0))

    @pl.when(jnp.logical_not((err <= FINE) & (lowest > 0.0)))
    def _():
        a_ref[...] = gn[...]
        y_ref[...] = one

        def pivot(k, _):
            col = jnp.sum(jnp.where(lane == k, a_ref[...], 0.0), axis=1, keepdims=True)
            row = jnp.sum(jnp.where(sub == k, a_ref[...], 0.0), axis=0, keepdims=True)
            yrow = jnp.sum(jnp.where(sub == k, y_ref[...], 0.0), axis=0, keepdims=True)
            top = jnp.sum(jnp.where(lax.broadcasted_iota(jnp.int32, (1, rank), 1) == k, row, 0.0))
            inv = 1.0 / jnp.sqrt(jnp.full((1, rank), top))
            row, yrow = row * inv, yrow * inv
            col = jnp.where(lax.broadcasted_iota(jnp.int32, (rank, 1), 0) > k, col * inv[:, :1], 0.0)
            a_ref[...] = a_ref[...] - col * row
            y_ref[...] = jnp.where(sub == k, yrow, y_ref[...] - col * yrow)
            return 0

        lax.fori_loop(0, rank, pivot, 0)

    xh, xl = halves(y_ref[...] * d_row)
    root = math.sqrt(rows)
    c = nt(mh[...], xh) + nt(mh[...], xl)
    c_up = (c[:rank] * root).astype(BF16)
    c_low = ((c[rank:] + nt(m_low, xh)) * root).astype(BF16)
    r = nt(hm_high, xh) + nt(hm_high, xl) + nt(hm_low, xh)
    r_up = jnp.where(sub < old, r[:rank], 0.0).astype(BF16)
    w_high, w_low = halves(r[rank:])
    r_low = (-(nn(kt[...], w_high) + nn(kt[...], w_low))).astype(BF16)
    step = rows // q_sem.shape[0]
    stores = []
    for t in range(rows // step):
        at = pl.ds(t * step, step)
        u, v = u_ref[at, :], v_ref[at, :]
        ui, uj = uit_ref[:, at], ujt[:, at]
        q_ref[at, :] = (nn(u, c_up) + tn(ui, c_low)).astype(BF16)
        stores.append(pltpu.make_async_copy(q_ref.at[at], q_hbm.at[at], q_sem.at[t]))
        stores[-1].start()
        w_ref[at, :] = (nn(v, r_up) + tn(uj, r_low)).astype(BF16)
        stores.append(pltpu.make_async_copy(w_ref.at[at], w_hbm.at[at], w_sem.at[t]))
        stores[-1].start()
    for copy in stores:
        copy.wait()


def body(tile_basis, tile_coeffs, panel_basis, panel_coeffs, tile_rank, target_rank, panel_rank, owner_row):
    n_row, n_col = lax.axis_size("row"), lax.axis_size("col")
    u, v = tile_basis[0, 0], tile_coeffs[0, 0]
    pu, pv = panel_basis[0], panel_coeffs[0]
    rows, rank = u.shape

    lefts, rights = {0: pu}, {0: pv}

    def grow(have, bits):
        for bit in bits:
            for m in list(have):
                have[m | bit] = swap(have[m], "col", n_col, bit)
        return tuple(have.values())

    high = [n_col >> t for t in range(1, n_col.bit_length() - 1)]

    gates = {
        0: lambda s: grow(lefts, high) if s == 2 else (),
        1: lambda _: grow(rights, high),
        n_row // 2: lambda _: grow(lefts, [1]) + grow(rights, [1]),
    }
    us, vs = ring_gathers(pu, pv, "row", n_row, gates)
    ui_parts = [lefts[m] for m in range(n_col)]

    ujs = picked_left(us, owner_row, n_row, n_col)
    ujs = [ujs[0]] + [swap(ujs[m], "col", n_col, m) for m in range(1, n_col)]
    kts = coupled(vs, [rights[m] for m in range(n_col)], owner_row, n_row, n_col)
    early = gram_products(tile_rank, target_rank, u, v, [after(ui_parts[0], kts[0]), *ui_parts[1:]])
    kts = [kts[0]] + [swap(kts[m], "col", n_col, m) for m in range(1, n_col)]

    out = jax.ShapeDtypeStruct((rows, rank), BF16)
    square = pltpu.VMEM((rank, rank), F32)
    tall, wide = pltpu.VMEM((rows, rank), BF16), pltpu.VMEM((rank, rows), BF16)
    tiles = rows // 384 if rows % 384 == 0 else 1
    fresh_basis, fresh_coeffs = pl.pallas_call(
        functools.partial(finish, n_col),
        out_shape=(out, out),
        in_specs=[SMEM] * 4 + [VMEM] * (8 + 2 * n_col),
        out_specs=(HBM, HBM),
        scratch_shapes=[
            wide,
            tall,
            tall,
            pltpu.VMEM((rank, rank), BF16),
            pltpu.VMEM((2 * rank, rank), BF16),
            square,
            square,
            square,
            pltpu.SemaphoreType.DMA((tiles,)),
            pltpu.SemaphoreType.DMA((tiles,)),
        ],
        compiler_params=pltpu.CompilerParams(vmem_limit_bytes=24 << 20),
        cost_estimate=pl.CostEstimate(flops=8 << 30, bytes_accessed=12 << 20, transcendentals=0),
        name="finish",
    )(tile_rank, target_rank, panel_rank, owner_row, u, v, *early, *ujs, *kts)
    return fresh_basis[None, None], fresh_coeffs[None, None]


def solution(mesh):
    tiles, panels = P("row", "col", None, None), P("row", "col", None)
    return jax.shard_map(
        body,
        mesh=mesh,
        in_specs=(tiles, tiles, panels, panels, P("row", "col"), P("row", "col"), P(), P()),
        out_specs=(tiles, tiles),
        check_vma=False,
    )
```
